32 devices in a mesh: stn: 4 (over y, x), freq: 8 (over z, core).
Axes of the slice: x: 2, y: 2, z: 4, core: 2. Of those that a mesh axis runs over, the one named last changes fastest.
Arguments:
- voltages: bfloat16 [512, 2, 8, 2, 5376], P(('stn', 'freq')), may hold values from -6 to 6
- filter_taps: float32 [12, 256], replicated, may hold values from -1.75 to 1.75
- beam_weights: bfloat16 [8, 2, 512, 1024], P('freq', None, 'stn'), may hold values from -0.25 to 0.25
- station_map: int32 [512], P('stn'), may hold values from 0 to 511, each once
- active_counts: int32 [8], P('freq'), may hold values from 256 to 512
Outputs:
- beams: bfloat16 [1024, 2, 8, 5120], P('stn', None, 'freq')
The draws below stay inside these ranges and needn't reach their ends.
Inputs may be any that keep to these rules, and one draw needn't show every extreme that they name: `station_map`: each station id appears in exactly one slot. `active_counts`: stations whose id is below the entry are active in that coarse channel.
All inputs are finite; a program needn't handle non-finite values.
Results may differ from the reference program's by a relative error of at most 0.0062.
Values may be sent and summed in bfloat16 or wider, within the bound.
No kernel may reach another device: no remote copies, remote signals or barrier semaphores. Data moves between devices by JAX's collectives and lax.ppermute only.
A program may use at most 192 MiB of HBM per device.

```python
import jax
import jax.numpy as jnp
from jax import lax

S = 512
POL = 2
F = 256
TAPS = 12
BEAMS = 1024
M = 10
C = 8


def touch_ends(array, own_key, low, high):
    dims = array.shape
    place = [jax.random.randint(jax.random.fold_in(own_key, axis), (), 0, dims[axis]) for axis in range(len(dims))]
    array = array.at[tuple(place)].set(low)
    longest = dims.index(max(dims))
    place[longest] = (place[longest] + 1) % dims[longest]
    return array.at[tuple(place)].set(high)


def strengthened(array, key, source, target, blocks, factor):
    def block_of(position):
        return (jnp.arange(array.shape[position]) // (array.shape[position] // blocks)).reshape((-1,) + (1,) * (array.ndim - 1 - position))

    first = jax.random.permutation(key, blocks)[block_of(target)]
    far = (block_of(target) + blocks // 2) % blocks
    return jnp.where((block_of(source) == first) | (block_of(source) == far), factor * array, array)


def shard_levels(own_key, extent, cuts, least, largest):
    level = 1.0
    for axis_at, parts in cuts:
        steps = jax.random.uniform(jax.random.fold_in(jax.random.fold_in(own_key, 6), axis_at), (parts,), jnp.float32, least / len(cuts), largest / len(cuts))
        level = level * jnp.repeat(jnp.exp(steps), extent[axis_at] // parts).reshape((-1,) + (1,) * (len(extent) - 1 - axis_at))
    return level


def normal_values(key, extent, width, bound, split=(), kind=jnp.bfloat16):
    entries = jax.random.normal(key, extent, jnp.float32) * width
    if len(split) > 0:
        entries = shard_levels(key, extent, split, -0.22, 0.18) * entries
    return jnp.clip(entries, min=-bound, max=bound).astype(kind)


def noise_with(key, extent, spread, reach, shards, heavy, kind=jnp.bfloat16):
    values = spread * jax.random.normal(key, extent, jnp.float32)
    if shards:
        values = values * shard_levels(key, extent, shards, -0.22, 0.18)
    return jnp.clip(strengthened(values, jax.random.fold_in(key, 3), *heavy), -reach, reach).astype(kind)


def setup_inputs(seed: int = 0) -> dict:
    arg_keys = jax.random.split(jax.random.key(seed), 6)
    return {
        "voltages": normal_values(arg_keys[0], (S, POL, C, 2, (M + TAPS - 1) * F), 1.0, 6.0, ((0, 32),)),
        "filter_taps": normal_values(arg_keys[1], (TAPS, F), TAPS ** -0.5, 1.75, (), jnp.float32),
        "beam_weights": noise_with(arg_keys[2], (C, 2, S, BEAMS), (2 * S) ** -0.5, 0.25, ((0, 8), (2, 4)), (2, 3, 4, 2.0)),
        "station_map": jax.random.permutation(arg_keys[3], S).astype(jnp.int32),
        "active_counts": touch_ends(jax.random.randint(arg_keys[4], (C,), S // 2, S + 1), jax.random.fold_in(arg_keys[4], 1), S // 2, S).astype(jnp.int32),
    }


def dft_table(fine):
    index = jnp.arange(fine, dtype=jnp.int32)
    phase = (index[:, None] * index[None, :]) % fine
    angle = phase.astype(jnp.float32) * (2.0 * jnp.pi / fine)
    factor = fine ** -0.5
    cosine = jnp.cos(angle) * factor
    sine = jnp.sin(angle) * factor
    upper = jnp.concatenate([cosine, -sine], axis=1)
    lower = jnp.concatenate([sine, cosine], axis=1)
    return jnp.concatenate([upper, lower], axis=0).astype(jnp.bfloat16)


def build_weights(masked):
    real_part = masked[:, 0]
    imag_part = masked[:, 1]
    real_row = jnp.concatenate([real_part, -imag_part], axis=1)
    imag_row = jnp.concatenate([imag_part, real_part], axis=1)
    return jnp.stack([real_row, imag_row], axis=2)


def reference(voltages, filter_taps, beam_weights, station_map, active_counts):
    frames = voltages.reshape(S, POL, C, 2, M + TAPS - 1, F)
    polyphase = jnp.zeros((S, POL, C, 2, M, F), jnp.float32)
    for tap in range(TAPS):
        polyphase = polyphase + filter_taps[tap].astype(jnp.float32) * frames[:, :, :, :, tap:tap + M, :].astype(jnp.float32)
    polyphase = polyphase.astype(jnp.bfloat16)
    inputs = polyphase.transpose(0, 1, 2, 4, 3, 5).reshape(S * POL * C * M, 2 * F)
    spectra = jnp.dot(inputs, dft_table(F), preferred_element_type=jnp.float32).astype(jnp.bfloat16)
    spectra = spectra.reshape(S, POL, C, M, 2, F)
    xmat = spectra.transpose(2, 4, 0, 1, 3, 5).reshape(C, 2 * S, POL * M * F)
    mask = (station_map[None, :] < active_counts[:, None]).astype(jnp.bfloat16)
    masked = beam_weights * mask[:, None, :, None]
    wbig = build_weights(masked)

    def one_channel(items):
        weights, data = items
        return jnp.einsum("kob,kr->bor", weights.astype(jnp.float32), data.astype(jnp.float32)).astype(jnp.bfloat16)

    result = lax.map(one_channel, (wbig, xmat))
    return result.transpose(1, 2, 0, 3)
```

```python
import functools

import jax
import jax.numpy as jnp
import numpy as np
from jax import lax
from jax.experimental import pallas as pl
from jax.experimental.layout import Layout, with_layout_constraint
from jax.experimental.pallas import tpu as pltpu
from jax.sharding import PartitionSpec as P


LANES = 128


def dft_table(fine):
    index = jnp.arange(fine, dtype=jnp.int32)
    phase = index[:, None] * index[None, :] % fine
    angle = phase.astype(jnp.float32) * (2.0 * jnp.pi / fine)
    factor = fine ** (-0.5)
    cosine = jnp.cos(angle) * factor
    sine = jnp.sin(angle) * factor
    upper = jnp.concatenate([cosine, -sine], axis=1)
    lower = jnp.concatenate([sine, cosine], axis=1)
    return jnp.concatenate([upper, lower], axis=0).astype(jnp.bfloat16)


def build_weights(masked):
    real_part = masked[:, 0]
    imag_part = masked[:, 1]
    real_row = jnp.concatenate([real_part, -imag_part], axis=1)
    imag_row = jnp.concatenate([imag_part, real_part], axis=1)
    return jnp.stack([real_row, imag_row], axis=2)


def plain(voltages, filter_taps, beam_weights, station_map, active_counts):
    slots, polars, chans, _, samples = voltages.shape
    taps, fine = filter_taps.shape
    blocks = samples // fine
    frames_out = blocks - taps + 1
    frames = voltages.reshape(slots, polars, chans, 2, blocks, fine)
    polyphase = jnp.zeros((slots, polars, chans, 2, frames_out, fine), jnp.float32)
    for tap in range(taps):
        polyphase = polyphase + filter_taps[tap] * frames[
            :, :, :, :, tap : tap + frames_out, :
        ].astype(jnp.float32)
    polyphase = polyphase.astype(jnp.bfloat16)
    inputs = polyphase.transpose(0, 1, 2, 4, 3, 5).reshape(
        slots * polars * chans * frames_out, 2 * fine
    )
    spectra = jnp.dot(inputs, dft_table(fine), preferred_element_type=jnp.float32).astype(
        jnp.bfloat16
    )
    spectra = spectra.reshape(slots, polars, chans, frames_out, 2, fine)
    arranged = spectra.transpose(2, 4, 0, 1, 3, 5).reshape(
        chans, 2, slots, polars * frames_out * fine
    )
    turned = lax.all_to_all(arranged, "freq", split_axis=0, concat_axis=2, tiled=True)
    own_chans, _, group_slots, row_count = turned.shape
    mask = (station_map[None, :] < active_counts[:, None]).astype(jnp.bfloat16)
    masked = beam_weights * mask[:, None, :, None]
    all_weights = lax.all_to_all(masked, "stn", split_axis=3, concat_axis=2, tiled=True)
    piece = lax.all_gather(turned, "stn", axis=2, tiled=True)
    width = piece.shape[2]
    wbig = build_weights(all_weights)
    data = piece.reshape(own_chans, 2 * width, row_count)
    summed = jnp.einsum("ckob,ckr->bocr", wbig, data, preferred_element_type=jnp.float32)
    return summed.astype(jnp.bfloat16)


def cos_sin(fine):
    index = np.arange(fine)
    angle = 2.0 * np.pi * ((index[:, None] * index[None, :]) % fine) / fine
    both = np.concatenate([np.cos(angle), np.sin(angle)], axis=1) * fine ** (-0.5)
    return jnp.asarray(both.astype(np.float32)).astype(jnp.bfloat16)


def spectra_body(dims, info, volt, taps_ref, table, out0, out1, wide, rows):
    slots, taps, frames_out, per_pair, pitch = dims
    blocks = frames_out + taps - 1
    core = info[1]
    for s in range(slots):
        wide[pl.ds(s * pitch, per_pair), :] = volt[s, 0, 0].astype(jnp.float32)
    for turn, out in ((0, out0), (1, out1)):
        base = jnp.bitwise_xor(core, turn) * (per_pair // 2)
        for q in range(2):
            for half in range(2):
                lane = half * LANES
                coef = [taps_ref[t : t + 1, lane : lane + LANES] for t in range(taps)]
                data = [
                    wide[pl.ds(base + 2 * (2 * i + half) + q, slots, stride=pitch), :]
                    for i in range(blocks)
                ]
                for m in range(frames_out):
                    total = coef[0] * data[m]
                    for t in range(1, taps):
                        total = total + coef[t] * data[m + t]
                    col = q * 2 * LANES + lane
                    rows[m * slots : (m + 1) * slots, col : col + LANES] = total.astype(
                        jnp.bfloat16
                    )
        fine = 2 * LANES
        first = jnp.dot(rows[:, :fine], table[...], preferred_element_type=jnp.float32)
        second = jnp.dot(rows[:, fine:], table[...], preferred_element_type=jnp.float32)
        real = (first[:, :fine] + second[:, fine:]).astype(jnp.bfloat16)
        imag = (second[:, :fine] - first[:, fine:]).astype(jnp.bfloat16)
        for m in range(frames_out):
            span = slice(m * fine, (m + 1) * fine)
            out[0, :, span] = real[m * slots : (m + 1) * slots]
            out[1, :, span] = imag[m * slots : (m + 1) * slots]


def spectra_pair(info, view, filter_taps, table):
    slots, polars, pairs, per_pair, _ = view.shape
    taps, fine = filter_taps.shape
    frames_out = per_pair // 8 - taps + 1
    width = frames_out * fine
    pitch = per_pair
    shape = jax.ShapeDtypeStruct((2, slots, polars * width), jnp.bfloat16)
    out_spec = pl.BlockSpec((2, slots, width), lambda p, info: (0, 0, p))
    return pl.pallas_call(
        functools.partial(spectra_body, (slots, taps, frames_out, per_pair, pitch)),
        grid_spec=pltpu.PrefetchScalarGridSpec(
            num_scalar_prefetch=1,
            grid=(polars,),
            in_specs=[
                pl.BlockSpec(
                    (slots, 1, 1, per_pair, LANES), lambda p, info: (0, p, info[0], 0, 0)
                ),
                pl.BlockSpec((taps, fine), lambda p, info: (0, 0)),
                pl.BlockSpec((fine, 2 * fine), lambda p, info: (0, 0)),
            ],
            out_specs=[out_spec, out_spec],
            scratch_shapes=[
                pltpu.VMEM((slots * pitch, LANES), jnp.float32),
                pltpu.VMEM((frames_out * slots, 2 * fine), jnp.bfloat16),
            ],
        ),
        out_shape=[shape, shape],
        compiler_params=pltpu.CompilerParams(
            dimension_semantics=("arbitrary",), vmem_limit_bytes=32 << 20
        ),
        cost_estimate=pl.CostEstimate(
            flops=8 * 10**8, bytes_accessed=4 * 10**6, transcendentals=0
        ),
        name="spectra",
    )(info, view, filter_taps, table)


def beam_body(count, tile, pitch, weights, *refs):
    pieces, out, data, wide = refs[:count], refs[count], refs[count + 1], refs[count + 2]
    slots = pieces[0].shape[1]
    for i, piece in enumerate(pieces):
        for q in range(2):
            data[(2 * i + q) * slots : (2 * i + q + 1) * slots, :] = piece[q]
    beams = weights.shape[1]
    for q in range(2):
        part = jnp.dot(weights[q], data[...], preferred_element_type=jnp.float32)
        for j in range(tile // LANES):
            wide[pl.ds(2 * j + q, beams, stride=pitch), :] = part[
                :, j * LANES : (j + 1) * LANES
            ]
    high = 2 * tile // LANES
    for b in range(beams):
        out[b] = wide[pl.ds(b * pitch, high), :].astype(jnp.bfloat16)


def beam_sum(weights, pieces, tile):
    _, beams, depth = weights.shape
    _, slots, total = pieces[0].shape
    high = 2 * tile // LANES
    pitch = high
    return pl.pallas_call(
        functools.partial(beam_body, len(pieces), tile, pitch),
        grid=(total // tile,),
        in_specs=[pl.BlockSpec((2, beams, depth), lambda n: (0, 0, 0))]
        + [pl.BlockSpec((2, slots, tile), lambda n: (0, 0, n)) for _ in pieces],
        out_specs=pl.BlockSpec((beams, high, LANES), lambda n: (0, n, 0)),
        out_shape=jax.ShapeDtypeStruct((beams, 2 * total // LANES, LANES), jnp.bfloat16),
        scratch_shapes=[
            pltpu.VMEM((depth, tile), jnp.bfloat16),
            pltpu.VMEM((beams * pitch, LANES), jnp.float32),
        ],
        compiler_params=pltpu.CompilerParams(
            dimension_semantics=("arbitrary",), vmem_limit_bytes=48 << 20
        ),
        cost_estimate=pl.CostEstimate(
            flops=4 * beams * depth * total,
            bytes_accessed=2 * (depth * total + 2 * beams * total),
            transcendentals=0,
        ),
        name="beams",
    )(weights, *pieces)


def swap(array, axis, step, size):
    return lax.ppermute(array, axis, [(i, i ^ step) for i in range(size)])


def xor_order(array, me, size):
    bit = 1
    while bit < size:
        turned = array.reshape(
            array.shape[0], size // (2 * bit), 2, bit, *array.shape[2:]
        )[:, :, ::-1].reshape(array.shape)
        array = jnp.where((me & bit) != 0, turned, array)
        bit *= 2
    return array


def fast(stn, freq, voltages, filter_taps, beam_weights, station_map, active_counts):
    slots, polars, chans, _, samples = voltages.shape
    taps, fine = filter_taps.shape
    s_me = lax.axis_index("stn")
    f_me = lax.axis_index("freq")

    mask = (station_map < active_counts[0]).astype(jnp.bfloat16)
    masked = beam_weights[0] * mask[None, :, None]
    width = masked.shape[2] // stn
    masked = masked.reshape(2, freq, slots, stn * width)
    masked = xor_order(masked, f_me, freq)
    wparts = []
    for j in range(stn):
        part = lax.dynamic_slice_in_dim(masked, (s_me ^ j) * width, width, axis=3)
        wparts.append(part if j == 0 else swap(part, "stn", j, stn))

    view = with_layout_constraint(
        voltages.reshape(slots, polars, chans, 2, samples // LANES, LANES),
        Layout((0, 1, 2, 4, 3, 5)),
    )
    view = view.transpose(0, 1, 2, 4, 3, 5).reshape(
        slots, polars, chans // 2, 4 * samples // LANES, LANES
    )
    table = cos_sin(fine)
    own = []
    for jz in range(freq // 2):
        info = jnp.stack([(f_me >> 1) ^ jz, f_me & 1]).astype(jnp.int32)
        own += spectra_pair(info, view, filter_taps, table)
    held = [own[0]] + [swap(own[j], "freq", j, freq) for j in range(1, freq)]

    pieces, wlist = [], []
    bits = [1 << i for i in range(stn.bit_length() - 1)]
    for j in range(freq):
        have = {0: held[j]}
        for bit in bits if j % 2 == 0 else bits[::-1]:
            have.update({g ^ bit: swap(a, "stn", bit, stn) for g, a in have.items()})
        for g in range(stn):
            pieces.append(have[g])
            wlist.append((g, j))

    stacked = jnp.stack(wparts, axis=0)
    arranged = stacked.transpose(2, 0, 1, 3, 4)
    real_w = arranged * jnp.array([1, -1], jnp.bfloat16)[None, None, :, None, None]
    imag_w = arranged[:, :, ::-1]
    weights = jnp.stack([real_w.reshape(-1, width).T, imag_w.reshape(-1, width).T])

    out = beam_sum(weights, pieces, 1024)
    high = out.shape[1] // 2
    return out.reshape(width, high, 2, LANES).transpose(0, 2, 1, 3).reshape(
        width, 2, 1, high * LANES
    )


def solution(mesh):
    placed = (
        P(("stn", "freq"), None, None, None, None),
        P(),
        P("freq", None, "stn", None),
        P("stn"),
        P("freq"),
    )
    stn, freq = mesh.shape["stn"], mesh.shape["freq"]

    def per_device(voltages, filter_taps, beam_weights, station_map, active_counts):
        args = (voltages, filter_taps, beam_weights, station_map, active_counts)
        if voltages.shape[0] % 16 or active_counts.shape[0] != 1:
            return plain(*args)
        return fast(stn, freq, *args)

    return jax.shard_map(
        per_device,
        mesh=mesh,
        in_specs=placed,
        out_specs=P("stn", None, "freq", None),
        check_vma=False,
    )
```

```python
import functools

import jax
import jax.numpy as jnp
import numpy as np
from jax import lax
from jax.experimental import pallas as pl
from jax.experimental.layout import Layout, with_layout_constraint
from jax.experimental.pallas import tpu as pltpu
from jax.sharding import PartitionSpec as P


LANES = 128


def dft_table(fine):
    index = jnp.arange(fine, dtype=jnp.int32)
    phase = index[:, None] * index[None, :] % fine
    angle = phase.astype(jnp.float32) * (2.0 * jnp.pi / fine)
    factor = fine ** (-0.5)
    cosine = jnp.cos(angle) * factor
    sine = jnp.sin(angle) * factor
    upper = jnp.concatenate([cosine, -sine], axis=1)
    lower = jnp.concatenate([sine, cosine], axis=1)
    return jnp.concatenate([upper, lower], axis=0).astype(jnp.bfloat16)


def build_weights(masked):
    real_part = masked[:, 0]
    imag_part = masked[:, 1]
    real_row = jnp.concatenate([real_part, -imag_part], axis=1)
    imag_row = jnp.concatenate([imag_part, real_part], axis=1)
    return jnp.stack([real_row, imag_row], axis=2)


def plain(voltages, filter_taps, beam_weights, station_map, active_counts):
    slots, polars, chans, _, samples = voltages.shape
    taps, fine = filter_taps.shape
    blocks = samples // fine
    frames_out = blocks - taps + 1
    frames = voltages.reshape(slots, polars, chans, 2, blocks, fine)
    polyphase = jnp.zeros((slots, polars, chans, 2, frames_out, fine), jnp.float32)
    for tap in range(taps):
        polyphase = polyphase + filter_taps[tap] * frames[
            :, :, :, :, tap : tap + frames_out, :
        ].astype(jnp.float32)
    polyphase = polyphase.astype(jnp.bfloat16)
    inputs = polyphase.transpose(0, 1, 2, 4, 3, 5).reshape(
        slots * polars * chans * frames_out, 2 * fine
    )
    spectra = jnp.dot(inputs, dft_table(fine), preferred_element_type=jnp.float32).astype(
        jnp.bfloat16
    )
    spectra = spectra.reshape(slots, polars, chans, frames_out, 2, fine)
    arranged = spectra.transpose(2, 4, 0, 1, 3, 5).reshape(
        chans, 2, slots, polars * frames_out * fine
    )
    turned = lax.all_to_all(arranged, "freq", split_axis=0, concat_axis=2, tiled=True)
    own_chans, _, _, row_count = turned.shape
    mask = (station_map[None, :] < active_counts[:, None]).astype(jnp.bfloat16)
    masked = beam_weights * mask[:, None, :, None]
    all_weights = lax.all_to_all(masked, "stn", split_axis=3, concat_axis=2, tiled=True)
    piece = lax.all_gather(turned, "stn", axis=2, tiled=True)
    width = piece.shape[2]
    wbig = build_weights(all_weights)
    data = piece.reshape(own_chans, 2 * width, row_count)
    summed = jnp.einsum("ckob,ckr->bocr", wbig, data, preferred_element_type=jnp.float32)
    return summed.astype(jnp.bfloat16)


def cos_sin(fine):
    index = np.arange(fine)
    angle = 2.0 * np.pi * ((index[:, None] * index[None, :]) % fine) / fine
    both = np.concatenate([np.cos(angle), np.sin(angle)], axis=1) * fine ** (-0.5)
    return jnp.asarray(both.astype(np.float32)).astype(jnp.bfloat16)


def spectra_body(dims, info, volt, taps_ref, table, *refs):
    slots, taps, frames_out, per_pair, pitch, split = dims
    outs, wide, rows = refs[:-2], refs[-2], refs[-1]
    blocks = frames_out + taps - 1
    core = info[1]
    fine = 2 * LANES
    for s in range(slots):
        wide[pl.ds(s * pitch, per_pair), :] = volt[s, 0, 0].astype(jnp.float32)
    for turn in range(2):
        base = jnp.bitwise_xor(core, turn) * (per_pair // 2)
        for q in range(2):
            for half in range(2):
                lane = half * LANES
                coef = [taps_ref[t : t + 1, lane : lane + LANES] for t in range(taps)]
                data = [
                    wide[pl.ds(base + 2 * (2 * i + half) + q, slots, stride=pitch), :]
                    for i in range(blocks)
                ]
                for m in range(frames_out):
                    total = coef[0] * data[m]
                    for t in range(1, taps):
                        total = total + coef[t] * data[m + t]
                    col = q * fine + lane
                    rows[m * slots : (m + 1) * slots, col : col + LANES] = total.astype(
                        jnp.bfloat16
                    )
        first = jnp.dot(rows[:, :fine], table[...], preferred_element_type=jnp.float32)
        second = jnp.dot(rows[:, fine:], table[...], preferred_element_type=jnp.float32)
        real = (first[:, :fine] + second[:, fine:]).astype(jnp.bfloat16)
        imag = (second[:, :fine] - first[:, fine:]).astype(jnp.bfloat16)

        def put(out):
            for m in range(frames_out):
                span = slice(m * fine, (m + 1) * fine)
                out[0, :, span] = real[m * slots : (m + 1) * slots]
                out[1, :, span] = imag[m * slots : (m + 1) * slots]

        if not split:
            put(outs[turn])
        else:
            for p in range(len(outs) // 2):
                pl.when(pl.program_id(0) == p)(functools.partial(put, outs[2 * p + turn]))


def spectra_pair(info, view, filter_taps, table, split):
    slots, polars, _, per_pair, _ = view.shape
    taps, fine = filter_taps.shape
    frames_out = per_pair // 8 - taps + 1
    width = frames_out * fine
    pitch = per_pair + 1
    if split:
        shapes = [jax.ShapeDtypeStruct((2, slots, width), jnp.bfloat16)] * (2 * polars)
        out_specs = [pl.BlockSpec((2, slots, width), lambda p, info: (0, 0, 0))] * len(shapes)
    else:
        shapes = [jax.ShapeDtypeStruct((2, slots, polars * width), jnp.bfloat16)] * 2
        out_specs = [pl.BlockSpec((2, slots, width), lambda p, info: (0, 0, p))] * 2
    return pl.pallas_call(
        functools.partial(
            spectra_body, (slots, taps, frames_out, per_pair, pitch, split)
        ),
        grid_spec=pltpu.PrefetchScalarGridSpec(
            num_scalar_prefetch=1,
            grid=(polars,),
            in_specs=[
                pl.BlockSpec(
                    (slots, 1, 1, per_pair, LANES), lambda p, info: (0, p, info[0], 0, 0)
                ),
                pl.BlockSpec((taps, fine), lambda p, info: (0, 0)),
                pl.BlockSpec((fine, 2 * fine), lambda p, info: (0, 0)),
            ],
            out_specs=out_specs,
            scratch_shapes=[
                pltpu.VMEM((slots * pitch, LANES), jnp.float32),
                pltpu.VMEM((frames_out * slots, 2 * fine), jnp.bfloat16),
            ],
        ),
        out_shape=shapes,
        compiler_params=pltpu.CompilerParams(dimension_semantics=("arbitrary",)),
        cost_estimate=pl.CostEstimate(
            flops=8 * 10**8, bytes_accessed=4 * 10**6, transcendentals=0
        ),
        name="spectra",
    )(info, view, filter_taps, table)


def mask_body(info, ids, count, weights, *outs):
    slots = weights.shape[2]
    width = outs[0].shape[3]
    place = jnp.bitwise_xor(pl.program_id(0), info[1]) * slots
    row = lax.broadcasted_iota(jnp.int32, (slots, LANES), 0)
    mine = jnp.zeros((slots, LANES), jnp.int32)
    for s in range(slots):
        mine = jnp.where(row == s, ids[place + s], mine)
    live = (mine < count[0]).astype(jnp.float32)[:, :1]
    for d, out in enumerate(outs):
        start = pl.multiple_of(jnp.bitwise_xor(info[0], d) * width, width)
        for q in range(2):
            value = weights[q, 0, :, pl.ds(start, width)].astype(jnp.float32)
            out[q, 0] = (value * live).astype(jnp.bfloat16)


def mask_weights(info, ids, count, weights, stn):
    _, freq, slots, beams = weights.shape
    width = beams // stn
    shape = jax.ShapeDtypeStruct((2, freq, slots, width), jnp.bfloat16)
    return pl.pallas_call(
        mask_body,
        grid_spec=pltpu.PrefetchScalarGridSpec(
            num_scalar_prefetch=3,
            grid=(freq,),
            in_specs=[
                pl.BlockSpec(
                    (2, 1, slots, beams),
                    lambda j, info, ids, count: (0, jnp.bitwise_xor(j, info[1]), 0, 0),
                )
            ],
            out_specs=[
                pl.BlockSpec((2, 1, slots, width), lambda j, info, ids, count: (0, j, 0, 0))
            ]
            * stn,
        ),
        out_shape=[shape] * stn,
        compiler_params=pltpu.CompilerParams(dimension_semantics=("arbitrary",)),
        name="mask",
    )(info, ids, count, weights)


def turn_body(*refs):
    parts, out = refs[:-1], refs[-1]
    rows = parts[0].shape[1]
    for g, part in enumerate(parts):
        real = part[0].astype(jnp.float32).T
        imag = part[1].astype(jnp.float32).T
        lead = slice(2 * g * rows, (2 * g + 1) * rows)
        tail = slice((2 * g + 1) * rows, (2 * g + 2) * rows)
        out[0, :, lead] = real.astype(jnp.bfloat16)
        out[0, :, tail] = (-imag).astype(jnp.bfloat16)
        out[1, :, lead] = imag.astype(jnp.bfloat16)
        out[1, :, tail] = real.astype(jnp.bfloat16)


def turn_weights(parts):
    _, rows, width = parts[0].shape
    return pl.pallas_call(
        turn_body,
        out_shape=jax.ShapeDtypeStruct((2, width, 2 * len(parts) * rows), jnp.bfloat16),
        name="turn",
    )(*parts)


def beam_body(places, tile, pitch, aliased, weights, *refs):
    count = len(places)
    pieces = refs[:count]
    out, data, wide = refs[count + aliased :]
    slots = pieces[0].shape[1]
    span = data.shape[0] // (2 * (max(g for g, _ in places) + 1))
    for (g, j), piece in zip(places, pieces):
        for q in range(2):
            row = (2 * g + q) * span + j * slots
            data[row : row + slots, :] = piece[q]
    beams = weights.shape[1]
    for q in range(2):
        part = jnp.dot(weights[q], data[...], preferred_element_type=jnp.float32)
        for j in range(tile // LANES):
            wide[pl.ds(2 * j + q, beams, stride=pitch), :] = part[
                :, j * LANES : (j + 1) * LANES
            ]
    high = 2 * tile // LANES
    for b in range(beams):
        out[b] = wide[pl.ds(b * pitch, high), :].astype(jnp.bfloat16)


def beam_sum(weights, pieces, total, first, steps, tile, before):
    _, beams, depth = weights.shape
    slots = pieces[0][2].shape[1]
    high = 2 * tile // LANES
    pitch = high + 1
    specs = [pl.BlockSpec((2, beams, depth), lambda n: (0, 0, 0))]
    for _, _, piece in pieces:
        shift = first if piece.shape[2] == total else 0
        specs.append(
            pl.BlockSpec((2, slots, tile), functools.partial(lambda d, n: (0, 0, n + d), shift))
        )
    extra = [] if before is None else [before]
    specs += [pl.BlockSpec(memory_space=pl.ANY)] * len(extra)
    return pl.pallas_call(
        functools.partial(
            beam_body, [(g, j) for g, j, _ in pieces], tile, pitch, len(extra)
        ),
        grid=(steps,),
        in_specs=specs,
        out_specs=pl.BlockSpec((beams, high, LANES), lambda n: (0, n + first, 0)),
        out_shape=jax.ShapeDtypeStruct((beams, 2 * total // LANES, LANES), jnp.bfloat16),
        input_output_aliases={len(pieces) + 1: 0} if extra else {},
        scratch_shapes=[
            pltpu.VMEM((depth, tile), jnp.bfloat16),
            pltpu.VMEM((beams * pitch, LANES), jnp.float32),
        ],
        compiler_params=pltpu.CompilerParams(dimension_semantics=("arbitrary",)),
        cost_estimate=pl.CostEstimate(
            flops=4 * beams * depth * tile * steps,
            bytes_accessed=2 * (depth + 2 * beams) * tile * steps,
            transcendentals=0,
        ),
        name="beams",
    )(weights, *[piece for _, _, piece in pieces], *extra)


def swap(array, axis, step, size):
    return lax.ppermute(array, axis, [(i, i ^ step) for i in range(size)])


def fast(stn, freq, voltages, filter_taps, beam_weights, station_map, active_counts):
    slots, polars, chans, _, samples = voltages.shape
    taps, fine = filter_taps.shape
    s_me = lax.axis_index("stn")
    f_me = lax.axis_index("freq")

    info = jnp.stack([s_me, f_me]).astype(jnp.int32)
    grouped = beam_weights[0].reshape(2, freq, slots, beam_weights.shape[3])
    wparts = mask_weights(info, station_map, active_counts, grouped, stn)
    wparts = [wparts[0]] + [swap(wparts[d], "stn", d, stn) for d in range(1, stn)]
    weights = turn_weights([w.reshape(2, freq * slots, -1) for w in wparts])

    view = with_layout_constraint(
        voltages.reshape(slots, polars, chans, 2, samples // LANES, LANES),
        Layout((0, 1, 2, 4, 3, 5)),
    )
    view = view.transpose(0, 1, 2, 4, 3, 5).reshape(
        slots, polars, chans // 2, 4 * samples // LANES, LANES
    )
    table = cos_sin(fine)
    planes = freq // 2
    total = polars * (samples - (taps - 1) * fine)
    held = {}
    for jz in range(planes):
        split = jz == planes - 1
        place = jnp.stack([(f_me >> 1) ^ jz, f_me & 1]).astype(jnp.int32)
        made = spectra_pair(place, view, filter_taps, table, split)
        for i, piece in enumerate(made):
            j, p = 2 * jz + i % 2, i // 2
            held[j, p] = piece if j == 0 else swap(piece, "freq", j, freq)

    bits = [1 << i for i in range(stn.bit_length() - 1)]
    have = {}
    for (j, p), piece in held.items():
        have[j, p] = {0: piece}
        for bit in bits if j % 2 == 0 else bits[::-1]:
            have[j, p].update({g ^ bit: swap(a, "stn", bit, stn) for g, a in have[j, p].items()})

    tile = 4 * LANES
    steps = total // polars // tile
    out = None
    for p in range(polars):
        pieces = [
            (g, j, piece)
            for (j, part), group in have.items()
            for g, piece in group.items()
            if j < freq - 2 or part == p
        ]
        out = beam_sum(weights, pieces, total, p * steps, steps, tile, out)
    high = out.shape[1] // 2
    return out.reshape(out.shape[0], high, 2, LANES).transpose(0, 2, 1, 3).reshape(
        out.shape[0], 2, 1, high * LANES
    )


def solution(mesh):
    placed = (
        P(("stn", "freq"), None, None, None, None),
        P(),
        P("freq", None, "stn", None),
        P("stn"),
        P("freq"),
    )
    stn, freq = mesh.shape["stn"], mesh.shape["freq"]

    def per_device(voltages, filter_taps, beam_weights, station_map, active_counts):
        args = (voltages, filter_taps, beam_weights, station_map, active_counts)
        if voltages.shape[0] % 16 or active_counts.shape[0] != 1:
            return plain(*args)
        return fast(stn, freq, *args)

    return jax.shard_map(
        per_device,
        mesh=mesh,
        in_specs=placed,
        out_specs=P("stn", None, "freq", None),
        check_vma=False,
    )
```

```python
import functools

import jax
import jax.numpy as jnp
import numpy as np
from jax import lax
from jax.experimental import pallas as pl
from jax.experimental.layout import Layout, with_layout_constraint
from jax.experimental.pallas import tpu as pltpu
from jax.sharding import PartitionSpec as P


LANES = 128


def dft_table(fine):
    index = jnp.arange(fine, dtype=jnp.int32)
    phase = index[:, None] * index[None, :] % fine
    angle = phase.astype(jnp.float32) * (2.0 * jnp.pi / fine)
    factor = fine ** (-0.5)
    cosine = jnp.cos(angle) * factor
    sine = jnp.sin(angle) * factor
    upper = jnp.concatenate([cosine, -sine], axis=1)
    lower = jnp.concatenate([sine, cosine], axis=1)
    return jnp.concatenate([upper, lower], axis=0).astype(jnp.bfloat16)


def build_weights(masked):
    real_part = masked[:, 0]
    imag_part = masked[:, 1]
    real_row = jnp.concatenate([real_part, -imag_part], axis=1)
    imag_row = jnp.concatenate([imag_part, real_part], axis=1)
    return jnp.stack([real_row, imag_row], axis=2)


def plain(voltages, filter_taps, beam_weights, station_map, active_counts):
    slots, polars, chans, _, samples = voltages.shape
    taps, fine = filter_taps.shape
    blocks = samples // fine
    frames_out = blocks - taps + 1
    frames = voltages.reshape(slots, polars, chans, 2, blocks, fine)
    polyphase = jnp.zeros((slots, polars, chans, 2, frames_out, fine), jnp.float32)
    for tap in range(taps):
        polyphase = polyphase + filter_taps[tap] * frames[
            :, :, :, :, tap : tap + frames_out, :
        ].astype(jnp.float32)
    polyphase = polyphase.astype(jnp.bfloat16)
    inputs = polyphase.transpose(0, 1, 2, 4, 3, 5).reshape(
        slots * polars * chans * frames_out, 2 * fine
    )
    spectra = jnp.dot(inputs, dft_table(fine), preferred_element_type=jnp.float32).astype(
        jnp.bfloat16
    )
    spectra = spectra.reshape(slots, polars, chans, frames_out, 2, fine)
    arranged = spectra.transpose(2, 4, 0, 1, 3, 5).reshape(
        chans, 2, slots, polars * frames_out * fine
    )
    turned = lax.all_to_all(arranged, "freq", split_axis=0, concat_axis=2, tiled=True)
    own_chans, _, _, row_count = turned.shape
    mask = (station_map[None, :] < active_counts[:, None]).astype(jnp.bfloat16)
    masked = beam_weights * mask[:, None, :, None]
    all_weights = lax.all_to_all(masked, "stn", split_axis=3, concat_axis=2, tiled=True)
    piece = lax.all_gather(turned, "stn", axis=2, tiled=True)
    width = piece.shape[2]
    wbig = build_weights(all_weights)
    data = piece.reshape(own_chans, 2 * width, row_count)
    summed = jnp.einsum("ckob,ckr->bocr", wbig, data, preferred_element_type=jnp.float32)
    return summed.astype(jnp.bfloat16)


def cos_sin(fine):
    index = np.arange(fine)
    angle = 2.0 * np.pi * ((index[:, None] * index[None, :]) % fine) / fine
    both = np.concatenate([np.cos(angle), np.sin(angle)], axis=1) * fine ** (-0.5)
    return jnp.asarray(both.astype(np.float32)).astype(jnp.bfloat16)


def spectra_body(dims, info, volt, taps_ref, table, *refs):
    slots, taps, frames_out, per_pair, pitch, split = dims
    outs, wide, rows = refs[:-2], refs[-2], refs[-1]
    blocks = frames_out + taps - 1
    core = info[1] & 1
    fine = 2 * LANES
    for s in range(slots):
        wide[pl.ds(s * pitch, per_pair), :] = volt[s, 0, 0].astype(jnp.float32)
    for turn in range(2):
        base = jnp.bitwise_xor(core, turn) * (per_pair // 2)
        for q in range(2):
            for half in range(2):
                lane = half * LANES
                coef = [taps_ref[t : t + 1, lane : lane + LANES] for t in range(taps)]
                data = [
                    wide[pl.ds(base + 2 * (2 * i + half) + q, slots, stride=pitch), :]
                    for i in range(blocks)
                ]
                for m in range(frames_out):
                    total = coef[0] * data[m]
                    for t in range(1, taps):
                        total = total + coef[t] * data[m + t]
                    col = q * fine + lane
                    rows[m * slots : (m + 1) * slots, col : col + LANES] = total.astype(
                        jnp.bfloat16
                    )
        first = jnp.dot(rows[:, :fine], table[...], preferred_element_type=jnp.float32)
        second = jnp.dot(rows[:, fine:], table[...], preferred_element_type=jnp.float32)
        real = (first[:, :fine] + second[:, fine:]).astype(jnp.bfloat16)
        imag = (second[:, :fine] - first[:, fine:]).astype(jnp.bfloat16)

        def put(out):
            for m in range(frames_out):
                span = slice(m * fine, (m + 1) * fine)
                out[0, :, span] = real[m * slots : (m + 1) * slots]
                out[1, :, span] = imag[m * slots : (m + 1) * slots]

        if not split:
            put(outs[turn])
        else:
            for p in range(len(outs) // 2):
                pl.when(pl.program_id(0) == p)(functools.partial(put, outs[2 * p + turn]))


def spectra_pair(info, plane, view, filter_taps, table, split):
    slots, polars, _, per_pair, _ = view.shape
    taps, fine = filter_taps.shape
    frames_out = per_pair // 8 - taps + 1
    width = frames_out * fine
    pitch = per_pair + 1
    if split:
        shapes = [jax.ShapeDtypeStruct((2, slots, width), jnp.bfloat16)] * (2 * polars)
        out_specs = [pl.BlockSpec((2, slots, width), lambda p, info: (0, 0, 0))] * len(shapes)
    else:
        shapes = [jax.ShapeDtypeStruct((2, slots, polars * width), jnp.bfloat16)] * 2
        out_specs = [pl.BlockSpec((2, slots, width), lambda p, info: (0, 0, p))] * 2
    return pl.pallas_call(
        functools.partial(spectra_body, (slots, taps, frames_out, per_pair, pitch, split)),
        grid_spec=pltpu.PrefetchScalarGridSpec(
            num_scalar_prefetch=1,
            grid=(polars,),
            in_specs=[
                pl.BlockSpec(
                    (slots, 1, 1, per_pair, LANES), lambda p, info: (0, p, (info[1] >> 1) ^ plane, 0, 0)
                ),
                pl.BlockSpec((taps, fine), lambda p, info: (0, 0)),
                pl.BlockSpec((fine, 2 * fine), lambda p, info: (0, 0)),
            ],
            out_specs=out_specs,
            scratch_shapes=[
                pltpu.VMEM((slots * pitch, LANES), jnp.float32),
                pltpu.VMEM((frames_out * slots, 2 * fine), jnp.bfloat16),
            ],
        ),
        out_shape=shapes,
        compiler_params=pltpu.CompilerParams(dimension_semantics=("arbitrary",)),
        cost_estimate=pl.CostEstimate(
            flops=8 * 10**8, bytes_accessed=4 * 10**6, transcendentals=0
        ),
        name="spectra",
    )(info, view, filter_taps, table)


def mask_body(info, count, ids, weights, *refs):
    outs, live = refs[:-1], refs[-1]
    _, freq, slots, _ = weights.shape
    width = outs[0].shape[3]
    known = jnp.broadcast_to(ids[...], (LANES, ids.shape[1])).astype(jnp.float32).T
    live[...] = (known < count[0].astype(jnp.float32)).astype(jnp.float32)
    for j in range(freq):
        place = jnp.bitwise_xor(info[1], j)
        keep = live[pl.ds(pl.multiple_of(place * slots, slots), slots), :][:, :1]
        for d, out in enumerate(outs):
            start = pl.multiple_of(jnp.bitwise_xor(info[0], d) * width, width)
            for q in range(2):
                value = weights[q, place, :, pl.ds(start, width)].astype(jnp.float32)
                out[q, j] = (value * keep).astype(jnp.bfloat16)


def mask_weights(info, ids, count, weights, stn):
    _, freq, slots, beams = weights.shape
    shape = jax.ShapeDtypeStruct((2, freq, slots, beams // stn), jnp.bfloat16)
    smem = pl.BlockSpec(memory_space=pltpu.SMEM)
    vmem = pl.BlockSpec(memory_space=pltpu.VMEM)
    return pl.pallas_call(
        mask_body,
        in_specs=[smem, smem, vmem, vmem],
        out_specs=[vmem] * stn,
        out_shape=[shape] * stn,
        scratch_shapes=[pltpu.VMEM((freq * slots, LANES), jnp.float32)],
        name="mask",
    )(info, count, ids.reshape(1, freq * slots), weights)


def turn_body(cut, *refs):
    parts, outs = refs[:-2], refs[-2:]
    rows = parts[0].shape[1]
    for g, part in enumerate(parts):
        real = part[0].astype(jnp.float32).T.astype(jnp.bfloat16)
        imag = part[1].astype(jnp.float32).T.astype(jnp.bfloat16)
        for out, low, high in ((outs[0], 0, cut), (outs[1], cut, rows)):
            size = high - low
            lead = slice(2 * g * size, (2 * g + 1) * size)
            tail = slice((2 * g + 1) * size, (2 * g + 2) * size)
            out[0, :, lead] = real[:, low:high]
            out[0, :, tail] = -imag[:, low:high]
            out[1, :, lead] = imag[:, low:high]
            out[1, :, tail] = real[:, low:high]


def turn_weights(parts, cut):
    _, rows, width = parts[0].shape
    return pl.pallas_call(
        functools.partial(turn_body, cut),
        out_shape=[
            jax.ShapeDtypeStruct((2, width, 2 * len(parts) * size), jnp.bfloat16)
            for size in (cut, rows - cut)
        ],
        name="turn",
    )(*parts)


def gather_rows(places, pieces, data):
    slots = pieces[0].shape[1]
    span = data.shape[0] // (2 * (max(g for g, _ in places) + 1))
    low = min(j for _, j in places)
    for (g, j), piece in zip(places, pieces):
        for q in range(2):
            row = (2 * g + q) * span + (j - low) * slots
            data[row : row + slots, :] = piece[q]


def early_body(places, weights, *refs):
    pieces, out, data = refs[: len(places)], refs[-2], refs[-1]
    gather_rows(places, pieces, data)
    for q in range(2):
        out[q] = jnp.dot(weights[q], data[...], preferred_element_type=jnp.float32)


def late_body(places, tile, pitch, weights, partial, *refs):
    pieces = refs[: len(places)]
    out, data, wide = refs[len(places) :]
    gather_rows(places, pieces, data)
    beams = weights.shape[1]
    for q in range(2):
        part = partial[q] + jnp.dot(
            weights[q], data[...], preferred_element_type=jnp.float32
        )
        for j in range(tile // LANES):
            wide[pl.ds(2 * j + q, beams, stride=pitch), :] = part[
                :, j * LANES : (j + 1) * LANES
            ]
    high = 2 * tile // LANES
    for b in range(beams):
        out[b] = wide[pl.ds(b * pitch, high), :].astype(jnp.bfloat16)


def beam_specs(weights, pieces, tile):
    _, beams, depth = weights.shape
    _, slots, total = pieces[0][2].shape
    specs = [pl.BlockSpec((2, beams, depth), lambda n: (0, 0, 0))]
    parts = [pl.BlockSpec((2, slots, tile), lambda n: (0, 0, n))] * len(pieces)
    sum_spec = pl.BlockSpec((2, beams, tile), lambda n: (0, 0, n))
    cost = pl.CostEstimate(
        flops=4 * beams * depth * total,
        bytes_accessed=2 * (depth + 4 * beams) * total,
        transcendentals=0,
    )
    places = [(g, j) for g, j, _ in pieces]
    return beams, depth, total, specs, parts, sum_spec, cost, places


def beam_early(weights, pieces, tile):
    beams, depth, total, specs, parts, sum_spec, cost, places = beam_specs(
        weights, pieces, tile
    )
    return pl.pallas_call(
        functools.partial(early_body, places),
        grid=(total // tile,),
        in_specs=specs + parts,
        out_specs=sum_spec,
        out_shape=jax.ShapeDtypeStruct((2, beams, total), jnp.float32),
        scratch_shapes=[pltpu.VMEM((depth, tile), jnp.bfloat16)],
        compiler_params=pltpu.CompilerParams(dimension_semantics=("arbitrary",)),
        cost_estimate=cost,
        name="early",
    )(weights, *[piece for _, _, piece in pieces])


def beam_late(weights, partial, pieces, tile):
    beams, depth, total, specs, parts, sum_spec, cost, places = beam_specs(
        weights, pieces, tile
    )
    high = 2 * tile // LANES
    pitch = high + 1
    return pl.pallas_call(
        functools.partial(late_body, places, tile, pitch),
        grid=(total // tile,),
        in_specs=specs + [sum_spec] + parts,
        out_specs=pl.BlockSpec((beams, high, LANES), lambda n: (0, n, 0)),
        out_shape=jax.ShapeDtypeStruct((beams, 2 * total // LANES, LANES), jnp.bfloat16),
        scratch_shapes=[
            pltpu.VMEM((depth, tile), jnp.bfloat16),
            pltpu.VMEM((beams * pitch, LANES), jnp.float32),
        ],
        compiler_params=pltpu.CompilerParams(dimension_semantics=("arbitrary",)),
        cost_estimate=cost,
        name="late",
    )(weights, partial, *[piece for _, _, piece in pieces])


def swap(array, axis, step, size):
    return lax.ppermute(array, axis, [(i, i ^ step) for i in range(size)])


def fast(stn, freq, voltages, filter_taps, beam_weights, station_map, active_counts):
    slots, polars, chans, _, samples = voltages.shape
    _, fine = filter_taps.shape
    s_me = lax.axis_index("stn")
    f_me = lax.axis_index("freq")

    info = jnp.stack([s_me, f_me]).astype(jnp.int32)
    grouped = beam_weights[0].reshape(2, freq, slots, beam_weights.shape[3])
    wparts = mask_weights(info, station_map, active_counts, grouped, stn)
    wparts = [wparts[0]] + [swap(wparts[d], "stn", d, stn) for d in range(1, stn)]
    w_early, w_late = turn_weights(
        [w.reshape(2, freq * slots, -1) for w in wparts], (freq - 2) * slots
    )

    view = with_layout_constraint(
        voltages.reshape(slots, polars, chans, 2, samples // LANES, LANES),
        Layout((0, 1, 2, 4, 3, 5)),
    )
    view = view.transpose(0, 1, 2, 4, 3, 5).reshape(
        slots, polars, chans // 2, 4 * samples // LANES, LANES
    )
    table = cos_sin(fine)
    planes = freq // 2
    held = {}
    for jz in range(planes):
        split = False
        made = spectra_pair(info, jz, view, filter_taps, table, split)
        for i, piece in enumerate(made):
            j, p = 2 * jz + i % 2, i // 2
            held[j, p] = piece if j == 0 else swap(piece, "freq", j, freq)

    bits = [1 << i for i in range(stn.bit_length() - 1)]
    have = {}
    for (j, p), piece in held.items():
        have[j, p] = {0: piece}
        for bit in bits if j % 2 == 0 else bits[::-1]:
            have[j, p].update({g ^ bit: swap(a, "stn", bit, stn) for g, a in have[j, p].items()})

    every = [
        (g, j, piece) for (j, _), group in have.items() for g, piece in group.items()
    ]
    partial = beam_early(w_early, [e for e in every if e[1] < freq - 2], 4 * LANES)
    out = beam_late(w_late, partial, [e for e in every if e[1] >= freq - 2], 4 * LANES)
    high = out.shape[1] // 2
    return out.reshape(out.shape[0], high, 2, LANES).transpose(0, 2, 1, 3).reshape(
        out.shape[0], 2, 1, high * LANES
    )


def solution(mesh):
    placed = (
        P(("stn", "freq"), None, None, None, None),
        P(),
        P("freq", None, "stn", None),
        P("stn"),
        P("freq"),
    )
    stn, freq = mesh.shape["stn"], mesh.shape["freq"]

    def per_device(voltages, filter_taps, beam_weights, station_map, active_counts):
        args = (voltages, filter_taps, beam_weights, station_map, active_counts)
        if voltages.shape[0] % 16 or active_counts.shape[0] != 1:
            return plain(*args)
        return fast(stn, freq, *args)

    return jax.shard_map(
        per_device,
        mesh=mesh,
        in_specs=placed,
        out_specs=P("stn", None, "freq", None),
        check_vma=False,
    )
```

```python
import functools

import jax
import jax.numpy as jnp
import numpy as np
from jax import lax
from jax.experimental import pallas as pl
from jax.experimental.layout import Layout, with_layout_constraint
from jax.experimental.pallas import tpu as pltpu
from jax.sharding import PartitionSpec as P


LANES = 128
KERNEL_VMEM = 16 << 20
VMEM_WHOLE = pl.BlockSpec(memory_space=pltpu.VMEM)


def dft_table(fine):
    index = jnp.arange(fine, dtype=jnp.int32)
    phase = index[:, None] * index[None, :] % fine
    angle = phase.astype(jnp.float32) * (2.0 * jnp.pi / fine)
    factor = fine ** (-0.5)
    cosine = jnp.cos(angle) * factor
    sine = jnp.sin(angle) * factor
    upper = jnp.concatenate([cosine, -sine], axis=1)
    lower = jnp.concatenate([sine, cosine], axis=1)
    return jnp.concatenate([upper, lower], axis=0).astype(jnp.bfloat16)


def build_weights(masked):
    real_part = masked[:, 0]
    imag_part = masked[:, 1]
    real_row = jnp.concatenate([real_part, -imag_part], axis=1)
    imag_row = jnp.concatenate([imag_part, real_part], axis=1)
    return jnp.stack([real_row, imag_row], axis=2)


def plain(voltages, filter_taps, beam_weights, station_map, active_counts):
    slots, polars, chans, _, samples = voltages.shape
    taps, fine = filter_taps.shape
    blocks = samples // fine
    frames_out = blocks - taps + 1
    frames = voltages.reshape(slots, polars, chans, 2, blocks, fine)
    polyphase = jnp.zeros((slots, polars, chans, 2, frames_out, fine), jnp.float32)
    for tap in range(taps):
        polyphase = polyphase + filter_taps[tap] * frames[
            :, :, :, :, tap : tap + frames_out, :
        ].astype(jnp.float32)
    polyphase = polyphase.astype(jnp.bfloat16)
    inputs = polyphase.transpose(0, 1, 2, 4, 3, 5).reshape(
        slots * polars * chans * frames_out, 2 * fine
    )
    spectra = jnp.dot(inputs, dft_table(fine), preferred_element_type=jnp.float32).astype(
        jnp.bfloat16
    )
    spectra = spectra.reshape(slots, polars, chans, frames_out, 2, fine)
    arranged = spectra.transpose(2, 4, 0, 1, 3, 5).reshape(
        chans, 2, slots, polars * frames_out * fine
    )
    turned = lax.all_to_all(arranged, "freq", split_axis=0, concat_axis=2, tiled=True)
    own_chans, _, _, row_count = turned.shape
    mask = (station_map[None, :] < active_counts[:, None]).astype(jnp.bfloat16)
    masked = beam_weights * mask[:, None, :, None]
    all_weights = lax.all_to_all(masked, "stn", split_axis=3, concat_axis=2, tiled=True)
    piece = lax.all_gather(turned, "stn", axis=2, tiled=True)
    width = piece.shape[2]
    wbig = build_weights(all_weights)
    data = piece.reshape(own_chans, 2 * width, row_count)
    summed = jnp.einsum("ckob,ckr->bocr", wbig, data, preferred_element_type=jnp.float32)
    return summed.astype(jnp.bfloat16)


def cos_sin(fine):
    index = np.arange(fine)
    angle = 2.0 * np.pi * ((index[:, None] * index[None, :]) % fine) / fine
    both = np.concatenate([np.cos(angle), np.sin(angle)], axis=1) * fine ** (-0.5)
    return jnp.asarray(both.astype(np.float32)).astype(jnp.bfloat16)


def spectra_body(dims, info, volt, taps_ref, table, *refs):
    slots, taps, frames_out, per_pair, pitch, split = dims
    outs, wide, rows = refs[:-2], refs[-2], refs[-1]
    blocks = frames_out + taps - 1
    core = info[1] & 1
    fine = 2 * LANES
    for s in range(slots):
        wide[pl.ds(s * pitch, per_pair), :] = volt[s, 0, 0].astype(jnp.float32)
    for turn in range(2):
        base = jnp.bitwise_xor(core, turn) * (per_pair // 2)
        for q in range(2):
            for half in range(2):
                lane = half * LANES
                coef = [taps_ref[t : t + 1, lane : lane + LANES] for t in range(taps)]
                data = [
                    wide[pl.ds(base + 2 * (2 * i + half) + q, slots, stride=pitch), :]
                    for i in range(blocks)
                ]
                for m in range(frames_out):
                    total = coef[0] * data[m]
                    for t in range(1, taps):
                        total = total + coef[t] * data[m + t]
                    col = q * fine + lane
                    rows[m * slots : (m + 1) * slots, col : col + LANES] = total.astype(
                        jnp.bfloat16
                    )
        first = jnp.dot(rows[:, :fine], table[...], preferred_element_type=jnp.float32)
        second = jnp.dot(rows[:, fine:], table[...], preferred_element_type=jnp.float32)
        real = (first[:, :fine] + second[:, fine:]).astype(jnp.bfloat16)
        imag = (second[:, :fine] - first[:, fine:]).astype(jnp.bfloat16)

        def put(out):
            for m in range(frames_out):
                span = slice(m * fine, (m + 1) * fine)
                out[0, :, span] = real[m * slots : (m + 1) * slots]
                out[1, :, span] = imag[m * slots : (m + 1) * slots]

        if not split:
            put(outs[turn])
        else:
            for p in range(len(outs) // 2):
                pl.when(pl.program_id(0) == p)(functools.partial(put, outs[2 * p + turn]))


def spectra_pair(info, plane, view, filter_taps, table, split):
    slots, polars, _, per_pair, _ = view.shape
    taps, fine = filter_taps.shape
    frames_out = per_pair // 8 - taps + 1
    width = frames_out * fine
    pitch = per_pair + 1
    if split:
        shapes = [jax.ShapeDtypeStruct((2, slots, width), jnp.bfloat16)] * (2 * polars)
        out_specs = [pl.BlockSpec((2, slots, width), lambda p, info: (0, 0, 0))] * len(shapes)
    else:
        shapes = [jax.ShapeDtypeStruct((2, slots, polars * width), jnp.bfloat16)] * 2
        out_specs = [pl.BlockSpec((2, slots, width), lambda p, info: (0, 0, p))] * 2
    return pl.pallas_call(
        functools.partial(spectra_body, (slots, taps, frames_out, per_pair, pitch, split)),
        grid_spec=pltpu.PrefetchScalarGridSpec(
            num_scalar_prefetch=1,
            grid=(polars,),
            in_specs=[
                pl.BlockSpec(
                    (slots, 1, 1, per_pair, LANES), lambda p, info: (0, p, (info[1] >> 1) ^ plane, 0, 0)
                ),
                pl.BlockSpec((taps, fine), lambda p, info: (0, 0)),
                pl.BlockSpec((fine, 2 * fine), lambda p, info: (0, 0)),
            ],
            out_specs=out_specs,
            scratch_shapes=[
                pltpu.VMEM((slots * pitch, LANES), jnp.float32),
                pltpu.VMEM((frames_out * slots, 2 * fine), jnp.bfloat16),
            ],
        ),
        out_shape=shapes,
        compiler_params=pltpu.CompilerParams(
            dimension_semantics=("arbitrary",), vmem_limit_bytes=KERNEL_VMEM
        ),
        cost_estimate=pl.CostEstimate(
            flops=8 * 10**8, bytes_accessed=4 * 10**6, transcendentals=0
        ),
        name="spectra",
    )(info, view, filter_taps, table)


def mask_body(info, count, ids, weights, *refs):
    outs, live = refs[:-1], refs[-1]
    _, freq, slots, _ = weights.shape
    width = outs[0].shape[3]
    known = jnp.broadcast_to(ids[...], (LANES, ids.shape[1])).astype(jnp.float32).T
    live[...] = (known < count[0].astype(jnp.float32)).astype(jnp.float32)
    for j in range(freq):
        place = jnp.bitwise_xor(info[1], j)
        keep = live[pl.ds(pl.multiple_of(place * slots, slots), slots), :][:, :1]
        for d, out in enumerate(outs):
            start = pl.multiple_of(jnp.bitwise_xor(info[0], d) * width, width)
            for q in range(2):
                value = weights[q, place, :, pl.ds(start, width)].astype(jnp.float32)
                out[q, j] = (value * keep).astype(jnp.bfloat16)


def mask_weights(info, ids, count, weights, stn):
    _, freq, slots, beams = weights.shape
    shape = jax.ShapeDtypeStruct((2, freq, slots, beams // stn), jnp.bfloat16)
    smem = pl.BlockSpec(memory_space=pltpu.SMEM)
    vmem = pl.BlockSpec(memory_space=pltpu.VMEM)
    return pl.pallas_call(
        mask_body,
        in_specs=[smem, smem, vmem, vmem],
        out_specs=[vmem] * stn,
        out_shape=[shape] * stn,
        scratch_shapes=[pltpu.VMEM((freq * slots, LANES), jnp.float32)],
        compiler_params=pltpu.CompilerParams(vmem_limit_bytes=KERNEL_VMEM),
        name="mask",
    )(info, count, ids.reshape(1, freq * slots), weights)


def turn_body(cut, *refs):
    parts, outs = refs[:-2], refs[-2:]
    rows = parts[0].shape[1]
    for g, part in enumerate(parts):
        real = part[0].astype(jnp.float32).T.astype(jnp.bfloat16)
        imag = part[1].astype(jnp.float32).T.astype(jnp.bfloat16)
        for out, low, high in ((outs[0], 0, cut), (outs[1], cut, rows)):
            size = high - low
            lead = slice(2 * g * size, (2 * g + 1) * size)
            tail = slice((2 * g + 1) * size, (2 * g + 2) * size)
            out[0, :, lead] = real[:, low:high]
            out[0, :, tail] = -imag[:, low:high]
            out[1, :, lead] = imag[:, low:high]
            out[1, :, tail] = real[:, low:high]


def turn_weights(parts, cut):
    _, rows, width = parts[0].shape
    return pl.pallas_call(
        functools.partial(turn_body, cut),
        out_shape=[
            jax.ShapeDtypeStruct((2, width, 2 * len(parts) * size), jnp.bfloat16)
            for size in (cut, rows - cut)
        ],
        compiler_params=pltpu.CompilerParams(vmem_limit_bytes=KERNEL_VMEM),
        name="turn",
    )(*parts)


def gather_rows(places, pieces, here, data):
    slots = pieces[0].shape[1]
    span = data.shape[0] // (2 * (max(g for g, _ in places) + 1))
    low = min(j for _, j in places)
    for (g, j), piece in zip(places, pieces):
        for q in range(2):
            row = (2 * g + q) * span + (j - low) * slots
            data[row : row + slots, :] = piece[q, :, here]


def columns(tile):
    return pl.ds(pl.multiple_of(pl.program_id(0) * tile, tile), tile)


def early_body(places, tile, weights, *refs):
    pieces, out, data = refs[: len(places)], refs[-2], refs[-1]
    here = columns(tile)
    gather_rows(places, pieces, here, data)
    for q in range(2):
        out[q, :, here] = jnp.dot(
            weights[q], data[...], preferred_element_type=jnp.float32
        )


def late_body(places, tile, pitch, weights, partial, *refs):
    pieces = refs[: len(places)]
    out, data, wide = refs[len(places) :]
    here = columns(tile)
    gather_rows(places, pieces, here, data)
    beams = weights.shape[1]
    for q in range(2):
        part = partial[q, :, here] + jnp.dot(
            weights[q], data[...], preferred_element_type=jnp.float32
        )
        for j in range(tile // LANES):
            wide[pl.ds(2 * j + q, beams, stride=pitch), :] = part[
                :, j * LANES : (j + 1) * LANES
            ]
    high = 2 * tile // LANES
    for b in range(beams):
        out[b] = wide[pl.ds(b * pitch, high), :].astype(jnp.bfloat16)


def beam_early(weights, pieces, tile):
    _, beams, depth = weights.shape
    total = pieces[0][2].shape[2]
    return pl.pallas_call(
        functools.partial(early_body, [(g, j) for g, j, _ in pieces], tile),
        grid=(total // tile,),
        in_specs=[VMEM_WHOLE] * (1 + len(pieces)),
        out_specs=VMEM_WHOLE,
        out_shape=jax.ShapeDtypeStruct((2, beams, total), jnp.float32),
        scratch_shapes=[pltpu.VMEM((depth, tile), jnp.bfloat16)],
        compiler_params=pltpu.CompilerParams(
            dimension_semantics=("arbitrary",), vmem_limit_bytes=KERNEL_VMEM
        ),
        name="early",
    )(weights, *[piece for _, _, piece in pieces])


def beam_late(weights, partial, pieces, tile):
    _, beams, depth = weights.shape
    total = pieces[0][2].shape[2]
    high = 2 * tile // LANES
    pitch = high + 1
    return pl.pallas_call(
        functools.partial(late_body, [(g, j) for g, j, _ in pieces], tile, pitch),
        grid=(total // tile,),
        in_specs=[VMEM_WHOLE] * (2 + len(pieces)),
        out_specs=pl.BlockSpec((beams, high, LANES), lambda n: (0, n, 0)),
        out_shape=jax.ShapeDtypeStruct((beams, 2 * total // LANES, LANES), jnp.bfloat16),
        scratch_shapes=[
            pltpu.VMEM((depth, tile), jnp.bfloat16),
            pltpu.VMEM((beams * pitch, LANES), jnp.float32),
        ],
        compiler_params=pltpu.CompilerParams(
            dimension_semantics=("arbitrary",), vmem_limit_bytes=KERNEL_VMEM
        ),
        name="late",
    )(weights, partial, *[piece for _, _, piece in pieces])


def swap(array, axis, step, size):
    return lax.ppermute(array, axis, [(i, i ^ step) for i in range(size)])


def fast(stn, freq, voltages, filter_taps, beam_weights, station_map, active_counts):
    slots, polars, chans, _, samples = voltages.shape
    _, fine = filter_taps.shape
    s_me = lax.axis_index("stn")
    f_me = lax.axis_index("freq")

    info = jnp.stack([s_me, f_me]).astype(jnp.int32)
    grouped = beam_weights[0].reshape(2, freq, slots, beam_weights.shape[3])
    wparts = mask_weights(info, station_map, active_counts, grouped, stn)
    wparts = [wparts[0]] + [swap(wparts[d], "stn", d, stn) for d in range(1, stn)]
    w_early, w_late = turn_weights(
        [w.reshape(2, freq * slots, -1) for w in wparts], (freq - 2) * slots
    )

    view = with_layout_constraint(
        voltages.reshape(slots, polars, chans, 2, samples // LANES, LANES),
        Layout((0, 1, 2, 4, 3, 5)),
    )
    view = view.transpose(0, 1, 2, 4, 3, 5).reshape(
        slots, polars, chans // 2, 4 * samples // LANES, LANES
    )
    view = pltpu.with_memory_space_constraint(view, pltpu.HBM)
    table = cos_sin(fine)
    planes = freq // 2
    held = {}
    for jz in range(planes):
        split = False
        made = spectra_pair(info, jz, view, filter_taps, table, split)
        for i, piece in enumerate(made):
            j, p = 2 * jz + i % 2, i // 2
            held[j, p] = piece if j == 0 else swap(piece, "freq", j, freq)

    bits = [1 << i for i in range(stn.bit_length() - 1)]
    have = {}
    for (j, p), piece in held.items():
        have[j, p] = {0: piece}
        for bit in bits if j % 2 == 0 else bits[::-1]:
            have[j, p].update({g ^ bit: swap(a, "stn", bit, stn) for g, a in have[j, p].items()})

    every = [
        (g, j, piece) for (j, _), group in have.items() for g, piece in group.items()
    ]
    partial = beam_early(w_early, [e for e in every if e[1] < freq - 2], 4 * LANES)
    out = beam_late(w_late, partial, [e for e in every if e[1] >= freq - 2], 4 * LANES)
    high = out.shape[1] // 2
    return out.reshape(out.shape[0], high, 2, LANES).transpose(0, 2, 1, 3).reshape(
        out.shape[0], 2, 1, high * LANES
    )


def solution(mesh):
    placed = (
        P(("stn", "freq"), None, None, None, None),
        P(),
        P("freq", None, "stn", None),
        P("stn"),
        P("freq"),
    )
    stn, freq = mesh.shape["stn"], mesh.shape["freq"]

    def per_device(voltages, filter_taps, beam_weights, station_map, active_counts):
        args = (voltages, filter_taps, beam_weights, station_map, active_counts)
        if voltages.shape[0] % 16 or active_counts.shape[0] != 1:
            return plain(*args)
        return fast(stn, freq, *args)

    return jax.shard_map(
        per_device,
        mesh=mesh,
        in_specs=placed,
        out_specs=P("stn", None, "freq", None),
        check_vma=False,
    )
```

```python
import functools

import jax
import jax.numpy as jnp
import numpy as np
from jax import lax
from jax.experimental import pallas as pl
from jax.experimental.layout import Layout, with_layout_constraint
from jax.experimental.pallas import tpu as pltpu
from jax.sharding import PartitionSpec as P


LANES = 128
KERNEL_VMEM = 16 << 20
VMEM_WHOLE = pl.BlockSpec(memory_space=pltpu.VMEM)


def dft_table(fine):
    index = jnp.arange(fine, dtype=jnp.int32)
    phase = index[:, None] * index[None, :] % fine
    angle = phase.astype(jnp.float32) * (2.0 * jnp.pi / fine)
    factor = fine ** (-0.5)
    cosine = jnp.cos(angle) * factor
    sine = jnp.sin(angle) * factor
    upper = jnp.concatenate([cosine, -sine], axis=1)
    lower = jnp.concatenate([sine, cosine], axis=1)
    return jnp.concatenate([upper, lower], axis=0).astype(jnp.bfloat16)


def build_weights(masked):
    real_part = masked[:, 0]
    imag_part = masked[:, 1]
    real_row = jnp.concatenate([real_part, -imag_part], axis=1)
    imag_row = jnp.concatenate([imag_part, real_part], axis=1)
    return jnp.stack([real_row, imag_row], axis=2)


def plain(voltages, filter_taps, beam_weights, station_map, active_counts):
    slots, polars, chans, _, samples = voltages.shape
    taps, fine = filter_taps.shape
    blocks = samples // fine
    frames_out = blocks - taps + 1
    frames = voltages.reshape(slots, polars, chans, 2, blocks, fine)
    polyphase = jnp.zeros((slots, polars, chans, 2, frames_out, fine), jnp.float32)
    for tap in range(taps):
        polyphase = polyphase + filter_taps[tap] * frames[
            :, :, :, :, tap : tap + frames_out, :
        ].astype(jnp.float32)
    polyphase = polyphase.astype(jnp.bfloat16)
    inputs = polyphase.transpose(0, 1, 2, 4, 3, 5).reshape(
        slots * polars * chans * frames_out, 2 * fine
    )
    spectra = jnp.dot(inputs, dft_table(fine), preferred_element_type=jnp.float32).astype(
        jnp.bfloat16
    )
    spectra = spectra.reshape(slots, polars, chans, frames_out, 2, fine)
    arranged = spectra.transpose(2, 4, 0, 1, 3, 5).reshape(
        chans, 2, slots, polars * frames_out * fine
    )
    turned = lax.all_to_all(arranged, "freq", split_axis=0, concat_axis=2, tiled=True)
    own_chans, _, _, row_count = turned.shape
    mask = (station_map[None, :] < active_counts[:, None]).astype(jnp.bfloat16)
    masked = beam_weights * mask[:, None, :, None]
    all_weights = lax.all_to_all(masked, "stn", split_axis=3, concat_axis=2, tiled=True)
    piece = lax.all_gather(turned, "stn", axis=2, tiled=True)
    width = piece.shape[2]
    wbig = build_weights(all_weights)
    data = piece.reshape(own_chans, 2 * width, row_count)
    summed = jnp.einsum("ckob,ckr->bocr", wbig, data, preferred_element_type=jnp.float32)
    return summed.astype(jnp.bfloat16)


def cos_sin(fine):
    index = np.arange(fine)
    angle = 2.0 * np.pi * ((index[:, None] * index[None, :]) % fine) / fine
    both = np.concatenate([np.cos(angle), np.sin(angle)], axis=1) * fine ** (-0.5)
    return jnp.asarray(both.astype(np.float32)).astype(jnp.bfloat16)


def spectra_body(dims, plane, near, info, volt, taps_ref, table, out0, out1, wide, rows):
    taps, frames_out, per_pair, pitch, chunk = dims
    blocks = frames_out + taps - 1
    core = info[1] & 1
    fine = 2 * LANES
    polar = pl.program_id(0)
    for s in range(chunk):
        part = volt[s, 0, 0] if near else volt[s, polar, (info[1] >> 1) ^ plane]
        wide[pl.ds(s * pitch, per_pair), :] = part.astype(jnp.float32)
    for turn, out in ((0, out0), (1, out1)):
        base = jnp.bitwise_xor(core, turn) * (per_pair // 2)
        for q in range(2):
            for half in range(2):
                lane = half * LANES
                coef = [taps_ref[t : t + 1, lane : lane + LANES] for t in range(taps)]
                data = [
                    wide[pl.ds(base + 2 * (2 * i + half) + q, chunk, stride=pitch), :]
                    for i in range(blocks)
                ]
                for m in range(frames_out):
                    total = coef[0] * data[m]
                    for t in range(1, taps):
                        total = total + coef[t] * data[m + t]
                    col = q * fine + lane
                    rows[m * chunk : (m + 1) * chunk, col : col + LANES] = total.astype(
                        rows.dtype
                    )
        left, right = (
            rows[:, q * fine : (q + 1) * fine].astype(jnp.bfloat16) for q in range(2)
        )
        first = jnp.dot(left, table[...], preferred_element_type=jnp.float32)
        second = jnp.dot(right, table[...], preferred_element_type=jnp.float32)
        real = first[:, :fine] + second[:, fine:]
        imag = second[:, :fine] - first[:, fine:]
        for m in range(frames_out):
            lead = m * fine
            if not near:
                lead = pl.multiple_of(polar * (frames_out * fine) + lead, LANES)
            here = slice(m * chunk, (m + 1) * chunk)
            out[0, :, pl.ds(lead, fine)] = real[here].astype(jnp.bfloat16)
            out[1, :, pl.ds(lead, fine)] = imag[here].astype(jnp.bfloat16)


def spectra_pair(info, plane, view, filter_taps, table):
    slots, polars, _, per_pair, _ = view.shape
    taps, fine = filter_taps.shape
    frames_out = per_pair // 8 - taps + 1
    width = frames_out * fine
    pitch = per_pair + 1
    near = plane == 0
    shapes = [jax.ShapeDtypeStruct((2, slots, polars * width), jnp.bfloat16)] * 2
    if near:
        chunk = slots // 2
        keep = [pltpu.with_memory_space_constraint(x, pltpu.HBM) for x in (view, filter_taps, table)]
        grid = (polars, slots // chunk)
        in_specs = [
            pl.BlockSpec(
                (chunk, 1, 1, per_pair, LANES), lambda p, h, info: (h, p, info[1] >> 1, 0, 0)
            ),
            pl.BlockSpec((taps, fine), lambda p, h, info: (0, 0)),
            pl.BlockSpec((fine, 2 * fine), lambda p, h, info: (0, 0)),
        ]
        out_specs = [pl.BlockSpec((2, chunk, width), lambda p, h, info: (0, h, p))] * 2
        kind = jnp.float32
    else:
        chunk = slots
        keep = [view, filter_taps, table]
        grid = (polars,)
        in_specs = [VMEM_WHOLE] * 3
        out_specs = [VMEM_WHOLE] * 2
        kind = jnp.bfloat16
    return pl.pallas_call(
        functools.partial(
            spectra_body, (taps, frames_out, per_pair, pitch, chunk), plane, near
        ),
        grid_spec=pltpu.PrefetchScalarGridSpec(
            num_scalar_prefetch=1,
            grid=grid,
            in_specs=in_specs,
            out_specs=out_specs,
            scratch_shapes=[
                pltpu.VMEM((chunk * pitch, LANES), jnp.float32),
                pltpu.VMEM((frames_out * chunk, 2 * fine), kind),
            ],
        ),
        out_shape=shapes,
        compiler_params=pltpu.CompilerParams(
            dimension_semantics=("arbitrary",) * len(grid), vmem_limit_bytes=KERNEL_VMEM
        ),
        name="spectra",
    )(info, *keep)


def mask_body(info, count, ids, weights, *refs):
    outs, live = refs[:-1], refs[-1]
    _, freq, slots, _ = weights.shape
    width = outs[0].shape[3]
    known = jnp.broadcast_to(ids[...], (LANES, ids.shape[1])).astype(jnp.float32).T
    live[...] = (known < count[0].astype(jnp.float32)).astype(jnp.float32)
    for j in range(freq):
        place = jnp.bitwise_xor(info[1], j)
        keep = live[pl.ds(pl.multiple_of(place * slots, slots), slots), :][:, :1]
        for d, out in enumerate(outs):
            start = pl.multiple_of(jnp.bitwise_xor(info[0], d) * width, width)
            for q in range(2):
                value = weights[q, place, :, pl.ds(start, width)].astype(jnp.float32)
                out[q, j] = (value * keep).astype(jnp.bfloat16)


def mask_weights(info, ids, count, weights, stn):
    _, freq, slots, beams = weights.shape
    shape = jax.ShapeDtypeStruct((2, freq, slots, beams // stn), jnp.bfloat16)
    smem = pl.BlockSpec(memory_space=pltpu.SMEM)
    vmem = pl.BlockSpec(memory_space=pltpu.VMEM)
    return pl.pallas_call(
        mask_body,
        in_specs=[smem, smem, vmem, vmem],
        out_specs=[vmem] * stn,
        out_shape=[shape] * stn,
        scratch_shapes=[pltpu.VMEM((freq * slots, LANES), jnp.float32)],
        compiler_params=pltpu.CompilerParams(vmem_limit_bytes=KERNEL_VMEM),
        name="mask",
    )(info, count, ids.reshape(1, freq * slots), weights)


def turn_body(cut, *refs):
    parts, outs = refs[:-2], refs[-2:]
    rows = parts[0].shape[1]
    for g, part in enumerate(parts):
        real = part[0].astype(jnp.float32).T.astype(jnp.bfloat16)
        imag = part[1].astype(jnp.float32).T.astype(jnp.bfloat16)
        for out, low, high in ((outs[0], 0, cut), (outs[1], cut, rows)):
            size = high - low
            lead = slice(2 * g * size, (2 * g + 1) * size)
            tail = slice((2 * g + 1) * size, (2 * g + 2) * size)
            out[0, :, lead] = real[:, low:high]
            out[0, :, tail] = -imag[:, low:high]
            out[1, :, lead] = imag[:, low:high]
            out[1, :, tail] = real[:, low:high]


def turn_weights(parts, cut):
    _, rows, width = parts[0].shape
    return pl.pallas_call(
        functools.partial(turn_body, cut),
        out_shape=[
            jax.ShapeDtypeStruct((2, width, 2 * len(parts) * size), jnp.bfloat16)
            for size in (cut, rows - cut)
        ],
        compiler_params=pltpu.CompilerParams(vmem_limit_bytes=KERNEL_VMEM),
        name="turn",
    )(*parts)


def gather_rows(places, pieces, here, data):
    slots = pieces[0].shape[1]
    span = data.shape[0] // (2 * (max(g for g, _ in places) + 1))
    low = min(j for _, j in places)
    for (g, j), piece in zip(places, pieces):
        for q in range(2):
            row = (2 * g + q) * span + (j - low) * slots
            data[row : row + slots, :] = piece[q, :, here]


def columns(tile):
    return pl.ds(pl.multiple_of(pl.program_id(0) * tile, tile), tile)


def early_body(places, tile, weights, *refs):
    pieces, out, data = refs[: len(places)], refs[-2], refs[-1]
    here = columns(tile)
    gather_rows(places, pieces, here, data)
    for q in range(2):
        out[q, :, here] = jnp.dot(
            weights[q], data[...], preferred_element_type=jnp.float32
        )


def late_body(places, tile, pitch, weights, partial, *refs):
    pieces = refs[: len(places)]
    out, data, wide = refs[len(places) :]
    here = columns(tile)
    gather_rows(places, pieces, here, data)
    beams = weights.shape[1]
    for q in range(2):
        part = partial[q, :, here] + jnp.dot(
            weights[q], data[...], preferred_element_type=jnp.float32
        )
        for j in range(tile // LANES):
            wide[pl.ds(2 * j + q, beams, stride=pitch), :] = part[
                :, j * LANES : (j + 1) * LANES
            ]
    high = 2 * tile // LANES
    for b in range(beams):
        out[b] = wide[pl.ds(b * pitch, high), :].astype(jnp.bfloat16)


def beam_early(weights, pieces, tile):
    _, beams, depth = weights.shape
    total = pieces[0][2].shape[2]
    return pl.pallas_call(
        functools.partial(early_body, [(g, j) for g, j, _ in pieces], tile),
        grid=(total // tile,),
        in_specs=[VMEM_WHOLE] * (1 + len(pieces)),
        out_specs=VMEM_WHOLE,
        out_shape=jax.ShapeDtypeStruct((2, beams, total), jnp.float32),
        scratch_shapes=[pltpu.VMEM((depth, tile), jnp.bfloat16)],
        compiler_params=pltpu.CompilerParams(
            dimension_semantics=("arbitrary",), vmem_limit_bytes=KERNEL_VMEM
        ),
        name="early",
    )(weights, *[piece for _, _, piece in pieces])


def beam_late(weights, partial, pieces, tile):
    _, beams, depth = weights.shape
    total = pieces[0][2].shape[2]
    high = 2 * tile // LANES
    pitch = high + 1
    return pl.pallas_call(
        functools.partial(late_body, [(g, j) for g, j, _ in pieces], tile, pitch),
        grid=(total // tile,),
        in_specs=[VMEM_WHOLE] * (2 + len(pieces)),
        out_specs=pl.BlockSpec((beams, high, LANES), lambda n: (0, n, 0)),
        out_shape=jax.ShapeDtypeStruct((beams, 2 * total // LANES, LANES), jnp.bfloat16),
        scratch_shapes=[
            pltpu.VMEM((depth, tile), jnp.bfloat16),
            pltpu.VMEM((beams * pitch, LANES), jnp.float32),
        ],
        compiler_params=pltpu.CompilerParams(
            dimension_semantics=("arbitrary",), vmem_limit_bytes=KERNEL_VMEM
        ),
        name="late",
    )(weights, partial, *[piece for _, _, piece in pieces])


def swap(array, axis, step, size):
    return lax.ppermute(array, axis, [(i, i ^ step) for i in range(size)])


def fast(stn, freq, voltages, filter_taps, beam_weights, station_map, active_counts):
    slots, polars, chans, _, samples = voltages.shape
    _, fine = filter_taps.shape
    s_me = lax.axis_index("stn")
    f_me = lax.axis_index("freq")

    info = jnp.stack([s_me, f_me]).astype(jnp.int32)
    grouped = beam_weights[0].reshape(2, freq, slots, beam_weights.shape[3])
    wparts = mask_weights(info, station_map, active_counts, grouped, stn)
    wparts = [wparts[0]] + [swap(wparts[d], "stn", d, stn) for d in range(1, stn)]
    w_early, w_late = turn_weights(
        [w.reshape(2, freq * slots, -1) for w in wparts], (freq - 2) * slots
    )

    view = with_layout_constraint(
        voltages.reshape(slots, polars, chans, 2, samples // LANES, LANES),
        Layout((0, 1, 2, 4, 3, 5)),
    )
    view = view.transpose(0, 1, 2, 4, 3, 5).reshape(
        slots, polars, chans // 2, 4 * samples // LANES, LANES
    )
    table = cos_sin(fine)
    planes = freq // 2
    held = {}
    for jz in range(planes):
        made = spectra_pair(info, jz, view, filter_taps, table)
        for i, piece in enumerate(made):
            j, p = 2 * jz + i % 2, i // 2
            held[j, p] = piece if j == 0 else swap(piece, "freq", j, freq)

    bits = [1 << i for i in range(stn.bit_length() - 1)]
    have = {}
    for (j, p), piece in held.items():
        have[j, p] = {0: piece}
        for bit in bits if j % 2 == 0 else bits[::-1]:
            have[j, p].update({g ^ bit: swap(a, "stn", bit, stn) for g, a in have[j, p].items()})

    every = [
        (g, j, piece) for (j, _), group in have.items() for g, piece in group.items()
    ]
    partial = beam_early(w_early, [e for e in every if e[1] < freq - 2], 4 * LANES)
    out = beam_late(w_late, partial, [e for e in every if e[1] >= freq - 2], 20 * LANES)
    high = out.shape[1] // 2
    return out.reshape(out.shape[0], high, 2, LANES).transpose(0, 2, 1, 3).reshape(
        out.shape[0], 2, 1, high * LANES
    )


def solution(mesh):
    placed = (
        P(("stn", "freq"), None, None, None, None),
        P(),
        P("freq", None, "stn", None),
        P("stn"),
        P("freq"),
    )
    stn, freq = mesh.shape["stn"], mesh.shape["freq"]

    def per_device(voltages, filter_taps, beam_weights, station_map, active_counts):
        args = (voltages, filter_taps, beam_weights, station_map, active_counts)
        if voltages.shape[0] % 16 or active_counts.shape[0] != 1:
            return plain(*args)
        return fast(stn, freq, *args)

    return jax.shard_map(
        per_device,
        mesh=mesh,
        in_specs=placed,
        out_specs=P("stn", None, "freq", None),
        check_vma=False,
    )
```

```python
import functools

import jax
import jax.numpy as jnp
import numpy as np
from jax import lax
from jax.experimental import pallas as pl
from jax.experimental.layout import Layout, with_layout_constraint
from jax.experimental.pallas import tpu as pltpu
from jax.sharding import PartitionSpec as P


LANES = 128
KERNEL_VMEM = 16 << 20
VMEM_WHOLE = pl.BlockSpec(memory_space=pltpu.VMEM)


def dft_table(fine):
    index = jnp.arange(fine, dtype=jnp.int32)
    phase = index[:, None] * index[None, :] % fine
    angle = phase.astype(jnp.float32) * (2.0 * jnp.pi / fine)
    factor = fine ** (-0.5)
    cosine = jnp.cos(angle) * factor
    sine = jnp.sin(angle) * factor
    upper = jnp.concatenate([cosine, -sine], axis=1)
    lower = jnp.concatenate([sine, cosine], axis=1)
    return jnp.concatenate([upper, lower], axis=0).astype(jnp.bfloat16)


def build_weights(masked):
    real_part = masked[:, 0]
    imag_part = masked[:, 1]
    real_row = jnp.concatenate([real_part, -imag_part], axis=1)
    imag_row = jnp.concatenate([imag_part, real_part], axis=1)
    return jnp.stack([real_row, imag_row], axis=2)


def plain(voltages, filter_taps, beam_weights, station_map, active_counts):
    slots, polars, chans, _, samples = voltages.shape
    taps, fine = filter_taps.shape
    blocks = samples // fine
    frames_out = blocks - taps + 1
    frames = voltages.reshape(slots, polars, chans, 2, blocks, fine)
    polyphase = jnp.zeros((slots, polars, chans, 2, frames_out, fine), jnp.float32)
    for tap in range(taps):
        polyphase = polyphase + filter_taps[tap] * frames[
            :, :, :, :, tap : tap + frames_out, :
        ].astype(jnp.float32)
    polyphase = polyphase.astype(jnp.bfloat16)
    inputs = polyphase.transpose(0, 1, 2, 4, 3, 5).reshape(
        slots * polars * chans * frames_out, 2 * fine
    )
    spectra = jnp.dot(inputs, dft_table(fine), preferred_element_type=jnp.float32).astype(
        jnp.bfloat16
    )
    spectra = spectra.reshape(slots, polars, chans, frames_out, 2, fine)
    arranged = spectra.transpose(2, 4, 0, 1, 3, 5).reshape(
        chans, 2, slots, polars * frames_out * fine
    )
    turned = lax.all_to_all(arranged, "freq", split_axis=0, concat_axis=2, tiled=True)
    own_chans, _, _, row_count = turned.shape
    mask = (station_map[None, :] < active_counts[:, None]).astype(jnp.bfloat16)
    masked = beam_weights * mask[:, None, :, None]
    all_weights = lax.all_to_all(masked, "stn", split_axis=3, concat_axis=2, tiled=True)
    piece = lax.all_gather(turned, "stn", axis=2, tiled=True)
    width = piece.shape[2]
    wbig = build_weights(all_weights)
    data = piece.reshape(own_chans, 2 * width, row_count)
    summed = jnp.einsum("ckob,ckr->bocr", wbig, data, preferred_element_type=jnp.float32)
    return summed.astype(jnp.bfloat16)


def cos_sin(fine):
    index = np.arange(fine)
    angle = 2.0 * np.pi * ((index[:, None] * index[None, :]) % fine) / fine
    both = np.concatenate([np.cos(angle), np.sin(angle)], axis=1) * fine ** (-0.5)
    return jnp.asarray(both.astype(np.float32)).astype(jnp.bfloat16)


def spectra_body(dims, plane, near, info, volt, taps_ref, table, out0, out1, wide, rows):
    taps, frames_out, per_pair, pitch, chunk = dims
    blocks = frames_out + taps - 1
    core = info[1] & 1
    fine = 2 * LANES
    polar = pl.program_id(0)
    for s in range(chunk):
        part = volt[s, 0, 0] if near else volt[s, polar, (info[1] >> 1) ^ plane]
        wide[pl.ds(s * pitch, per_pair), :] = part.astype(jnp.float32)
    for turn, out in ((0, out0), (1, out1)):
        base = jnp.bitwise_xor(core, turn) * (per_pair // 2)
        for q in range(2):
            for half in range(2):
                lane = half * LANES
                coef = [taps_ref[t : t + 1, lane : lane + LANES] for t in range(taps)]
                data = [
                    wide[pl.ds(base + 2 * (2 * i + half) + q, chunk, stride=pitch), :]
                    for i in range(blocks)
                ]
                for m in range(frames_out):
                    total = coef[0] * data[m]
                    for t in range(1, taps):
                        total = total + coef[t] * data[m + t]
                    col = q * fine + lane
                    rows[m * chunk : (m + 1) * chunk, col : col + LANES] = total.astype(
                        rows.dtype
                    )
        first = jnp.dot(rows[:, :fine], table[...], preferred_element_type=jnp.float32)
        second = jnp.dot(rows[:, fine:], table[...], preferred_element_type=jnp.float32)
        real = first[:, :fine] + second[:, fine:]
        imag = second[:, :fine] - first[:, fine:]
        for m in range(frames_out):
            lead = pl.multiple_of((polar * frames_out + m) * fine, LANES)
            here = slice(m * chunk, (m + 1) * chunk)
            out[0, :, pl.ds(lead, fine)] = real[here].astype(jnp.bfloat16)
            out[1, :, pl.ds(lead, fine)] = imag[here].astype(jnp.bfloat16)


def spectra_pair(info, plane, view, filter_taps, table):
    slots, polars, _, per_pair, _ = view.shape
    taps, fine = filter_taps.shape
    frames_out = per_pair // 8 - taps + 1
    pitch = per_pair + 1
    near = plane == 0
    shapes = [jax.ShapeDtypeStruct((2, slots, polars * frames_out * fine), jnp.bfloat16)] * 2
    if near:
        keep = [pltpu.with_memory_space_constraint(x, pltpu.HBM) for x in (view, filter_taps, table)]
        in_specs = [
            pl.BlockSpec(
                (slots, 1, 1, per_pair, LANES), lambda p, info: (0, p, info[1] >> 1, 0, 0)
            ),
            pl.BlockSpec((taps, fine), lambda p, info: (0, 0)),
            pl.BlockSpec((fine, 2 * fine), lambda p, info: (0, 0)),
        ]
    else:
        keep = [view, filter_taps, table]
        in_specs = [VMEM_WHOLE] * 3
    return pl.pallas_call(
        functools.partial(
            spectra_body, (taps, frames_out, per_pair, pitch, slots), plane, near
        ),
        grid_spec=pltpu.PrefetchScalarGridSpec(
            num_scalar_prefetch=1,
            grid=(polars,),
            in_specs=in_specs,
            out_specs=[VMEM_WHOLE] * 2,
            scratch_shapes=[
                pltpu.VMEM((slots * pitch, LANES), jnp.float32),
                pltpu.VMEM((frames_out * slots, 2 * fine), jnp.bfloat16),
            ],
        ),
        out_shape=shapes,
        compiler_params=pltpu.CompilerParams(
            dimension_semantics=("arbitrary",), vmem_limit_bytes=KERNEL_VMEM
        ),
        name="spectra",
    )(info, *keep)


def mask_body(info, count, ids, weights, *refs):
    outs, live = refs[:-1], refs[-1]
    _, freq, slots, _ = weights.shape
    width = outs[0].shape[3]
    known = jnp.broadcast_to(ids[...], (LANES, ids.shape[1])).astype(jnp.float32).T
    live[...] = (known < count[0].astype(jnp.float32)).astype(jnp.float32)
    for j in range(freq):
        place = jnp.bitwise_xor(info[1], j)
        keep = live[pl.ds(pl.multiple_of(place * slots, slots), slots), :][:, :1]
        for d, out in enumerate(outs):
            start = pl.multiple_of(jnp.bitwise_xor(info[0], d) * width, width)
            for q in range(2):
                value = weights[q, place, :, pl.ds(start, width)].astype(jnp.float32)
                out[q, j] = (value * keep).astype(jnp.bfloat16)


def mask_weights(info, ids, count, weights, stn):
    _, freq, slots, beams = weights.shape
    shape = jax.ShapeDtypeStruct((2, freq, slots, beams // stn), jnp.bfloat16)
    smem = pl.BlockSpec(memory_space=pltpu.SMEM)
    vmem = pl.BlockSpec(memory_space=pltpu.VMEM)
    return pl.pallas_call(
        mask_body,
        in_specs=[smem, smem, vmem, vmem],
        out_specs=[vmem] * stn,
        out_shape=[shape] * stn,
        scratch_shapes=[pltpu.VMEM((freq * slots, LANES), jnp.float32)],
        compiler_params=pltpu.CompilerParams(vmem_limit_bytes=KERNEL_VMEM),
        name="mask",
    )(info, count, ids.reshape(1, freq * slots), weights)


def turn_body(cut, *refs):
    parts, outs = refs[:-2], refs[-2:]
    rows = parts[0].shape[1]
    for g, part in enumerate(parts):
        real = part[0].astype(jnp.float32).T.astype(jnp.bfloat16)
        imag = part[1].astype(jnp.float32).T.astype(jnp.bfloat16)
        for out, low, high in ((outs[0], 0, cut), (outs[1], cut, rows)):
            size = high - low
            lead = slice(2 * g * size, (2 * g + 1) * size)
            tail = slice((2 * g + 1) * size, (2 * g + 2) * size)
            out[0, :, lead] = real[:, low:high]
            out[0, :, tail] = -imag[:, low:high]
            out[1, :, lead] = imag[:, low:high]
            out[1, :, tail] = real[:, low:high]


def turn_weights(parts, cut):
    _, rows, width = parts[0].shape
    return pl.pallas_call(
        functools.partial(turn_body, cut),
        out_shape=[
            jax.ShapeDtypeStruct((2, width, 2 * len(parts) * size), jnp.bfloat16)
            for size in (cut, rows - cut)
        ],
        compiler_params=pltpu.CompilerParams(vmem_limit_bytes=KERNEL_VMEM),
        name="turn",
    )(*parts)


def gather_rows(places, pieces, here, data):
    slots = pieces[0].shape[1]
    span = data.shape[0] // (2 * (max(g for g, _ in places) + 1))
    low = min(j for _, j in places)
    for (g, j), piece in zip(places, pieces):
        for q in range(2):
            row = (2 * g + q) * span + (j - low) * slots
            data[row : row + slots, :] = piece[q, :, here]


def columns(tile):
    return pl.ds(pl.multiple_of(pl.program_id(0) * tile, tile), tile)


def early_body(places, tile, weights, *refs):
    pieces, out, data = refs[: len(places)], refs[-2], refs[-1]
    here = columns(tile)
    gather_rows(places, pieces, here, data)
    for q in range(2):
        out[q, :, here] = jnp.dot(
            weights[q], data[...], preferred_element_type=jnp.float32
        )


def late_body(places, tile, pitch, weights, partial, *refs):
    pieces = refs[: len(places)]
    out, data, wide = refs[len(places) :]
    here = columns(tile)
    gather_rows(places, pieces, here, data)
    beams = weights.shape[1]
    for q in range(2):
        part = partial[q, :, here] + jnp.dot(
            weights[q], data[...], preferred_element_type=jnp.float32
        )
        for j in range(tile // LANES):
            wide[pl.ds(2 * j + q, beams, stride=pitch), :] = part[
                :, j * LANES : (j + 1) * LANES
            ]
    high = 2 * tile // LANES
    for b in range(beams):
        out[b] = wide[pl.ds(b * pitch, high), :].astype(jnp.bfloat16)


def beam_early(weights, pieces, tile):
    _, beams, depth = weights.shape
    total = pieces[0][2].shape[2]
    return pl.pallas_call(
        functools.partial(early_body, [(g, j) for g, j, _ in pieces], tile),
        grid=(total // tile,),
        in_specs=[VMEM_WHOLE] * (1 + len(pieces)),
        out_specs=VMEM_WHOLE,
        out_shape=jax.ShapeDtypeStruct((2, beams, total), jnp.float32),
        scratch_shapes=[pltpu.VMEM((depth, tile), jnp.bfloat16)],
        compiler_params=pltpu.CompilerParams(
            dimension_semantics=("arbitrary",), vmem_limit_bytes=KERNEL_VMEM
        ),
        name="early",
    )(weights, *[piece for _, _, piece in pieces])


def beam_late(weights, partial, pieces, tile):
    _, beams, depth = weights.shape
    total = pieces[0][2].shape[2]
    high = 2 * tile // LANES
    pitch = high + 1
    return pl.pallas_call(
        functools.partial(late_body, [(g, j) for g, j, _ in pieces], tile, pitch),
        grid=(total // tile,),
        in_specs=[VMEM_WHOLE] * (2 + len(pieces)),
        out_specs=pl.BlockSpec((beams, high, LANES), lambda n: (0, n, 0)),
        out_shape=jax.ShapeDtypeStruct((beams, 2 * total // LANES, LANES), jnp.bfloat16),
        scratch_shapes=[
            pltpu.VMEM((depth, tile), jnp.bfloat16),
            pltpu.VMEM((beams * pitch, LANES), jnp.float32),
        ],
        compiler_params=pltpu.CompilerParams(
            dimension_semantics=("arbitrary",), vmem_limit_bytes=KERNEL_VMEM
        ),
        name="late",
    )(weights, partial, *[piece for _, _, piece in pieces])


def swap(array, axis, step, size):
    return lax.ppermute(array, axis, [(i, i ^ step) for i in range(size)])


def fast(stn, freq, voltages, filter_taps, beam_weights, station_map, active_counts):
    slots, polars, chans, _, samples = voltages.shape
    _, fine = filter_taps.shape
    s_me = lax.axis_index("stn")
    f_me = lax.axis_index("freq")

    info = jnp.stack([s_me, f_me]).astype(jnp.int32)
    grouped = beam_weights[0].reshape(2, freq, slots, beam_weights.shape[3])
    wparts = mask_weights(info, station_map, active_counts, grouped, stn)
    wparts = [wparts[0]] + [swap(wparts[d], "stn", d, stn) for d in range(1, stn)]
    w_early, w_late = turn_weights(
        [w.reshape(2, freq * slots, -1) for w in wparts], (freq - 2) * slots
    )

    view = with_layout_constraint(
        voltages.reshape(slots, polars, chans, 2, samples // LANES, LANES),
        Layout((0, 1, 2, 4, 3, 5)),
    )
    view = view.transpose(0, 1, 2, 4, 3, 5).reshape(
        slots, polars, chans // 2, 4 * samples // LANES, LANES
    )
    table = cos_sin(fine)
    planes = freq // 2
    held = {}
    for jz in range(planes):
        made = spectra_pair(info, jz, view, filter_taps, table)
        for i, piece in enumerate(made):
            j, p = 2 * jz + i % 2, i // 2
            held[j, p] = piece if j == 0 else swap(piece, "freq", j, freq)

    bits = [1 << i for i in range(stn.bit_length() - 1)]
    have = {}
    for (j, p), piece in held.items():
        have[j, p] = {0: piece}
        for bit in bits if j % 2 == 0 else bits[::-1]:
            have[j, p].update({g ^ bit: swap(a, "stn", bit, stn) for g, a in have[j, p].items()})

    every = [
        (g, j, piece) for (j, _), group in have.items() for g, piece in group.items()
    ]
    partial = beam_early(w_early, [e for e in every if e[1] < freq - 2], 4 * LANES)
    out = beam_late(w_late, partial, [e for e in every if e[1] >= freq - 2], 20 * LANES)
    high = out.shape[1] // 2
    return out.reshape(out.shape[0], high, 2, LANES).transpose(0, 2, 1, 3).reshape(
        out.shape[0], 2, 1, high * LANES
    )


def solution(mesh):
    placed = (
        P(("stn", "freq"), None, None, None, None),
        P(),
        P("freq", None, "stn", None),
        P("stn"),
        P("freq"),
    )
    stn, freq = mesh.shape["stn"], mesh.shape["freq"]

    def per_device(voltages, filter_taps, beam_weights, station_map, active_counts):
        args = (voltages, filter_taps, beam_weights, station_map, active_counts)
        if voltages.shape[0] % 16 or active_counts.shape[0] != 1:
            return plain(*args)
        return fast(stn, freq, *args)

    return jax.shard_map(
        per_device,
        mesh=mesh,
        in_specs=placed,
        out_specs=P("stn", None, "freq", None),
        check_vma=False,
    )
```

```python
import functools

import jax
import jax.numpy as jnp
import numpy as np
from jax import lax
from jax.experimental import pallas as pl
from jax.experimental.layout import Layout, with_layout_constraint
from jax.experimental.pallas import tpu as pltpu
from jax.sharding import PartitionSpec as P


LANES = 128
KERNEL_VMEM = 16 << 20
VMEM_WHOLE = pl.BlockSpec(memory_space=pltpu.VMEM)


def dft_table(fine):
    index = jnp.arange(fine, dtype=jnp.int32)
    phase = index[:, None] * index[None, :] % fine
    angle = phase.astype(jnp.float32) * (2.0 * jnp.pi / fine)
    factor = fine ** (-0.5)
    cosine = jnp.cos(angle) * factor
    sine = jnp.sin(angle) * factor
    upper = jnp.concatenate([cosine, -sine], axis=1)
    lower = jnp.concatenate([sine, cosine], axis=1)
    return jnp.concatenate([upper, lower], axis=0).astype(jnp.bfloat16)


def build_weights(masked):
    real_part = masked[:, 0]
    imag_part = masked[:, 1]
    real_row = jnp.concatenate([real_part, -imag_part], axis=1)
    imag_row = jnp.concatenate([imag_part, real_part], axis=1)
    return jnp.stack([real_row, imag_row], axis=2)


def plain(voltages, filter_taps, beam_weights, station_map, active_counts):
    slots, polars, chans, _, samples = voltages.shape
    taps, fine = filter_taps.shape
    blocks = samples // fine
    frames_out = blocks - taps + 1
    frames = voltages.reshape(slots, polars, chans, 2, blocks, fine)
    polyphase = jnp.zeros((slots, polars, chans, 2, frames_out, fine), jnp.float32)
    for tap in range(taps):
        polyphase = polyphase + filter_taps[tap] * frames[
            :, :, :, :, tap : tap + frames_out, :
        ].astype(jnp.float32)
    polyphase = polyphase.astype(jnp.bfloat16)
    inputs = polyphase.transpose(0, 1, 2, 4, 3, 5).reshape(
        slots * polars * chans * frames_out, 2 * fine
    )
    spectra = jnp.dot(inputs, dft_table(fine), preferred_element_type=jnp.float32).astype(
        jnp.bfloat16
    )
    spectra = spectra.reshape(slots, polars, chans, frames_out, 2, fine)
    arranged = spectra.transpose(2, 4, 0, 1, 3, 5).reshape(
        chans, 2, slots, polars * frames_out * fine
    )
    turned = lax.all_to_all(arranged, "freq", split_axis=0, concat_axis=2, tiled=True)
    own_chans, _, _, row_count = turned.shape
    mask = (station_map[None, :] < active_counts[:, None]).astype(jnp.bfloat16)
    masked = beam_weights * mask[:, None, :, None]
    all_weights = lax.all_to_all(masked, "stn", split_axis=3, concat_axis=2, tiled=True)
    piece = lax.all_gather(turned, "stn", axis=2, tiled=True)
    width = piece.shape[2]
    wbig = build_weights(all_weights)
    data = piece.reshape(own_chans, 2 * width, row_count)
    summed = jnp.einsum("ckob,ckr->bocr", wbig, data, preferred_element_type=jnp.float32)
    return summed.astype(jnp.bfloat16)


def cos_sin(fine):
    index = np.arange(fine)
    angle = 2.0 * np.pi * ((index[:, None] * index[None, :]) % fine) / fine
    both = np.concatenate([np.cos(angle), np.sin(angle)], axis=1) * fine ** (-0.5)
    return jnp.asarray(both.astype(np.float32)).astype(jnp.bfloat16)


def spectra_body(dims, plane, near, info, volt, taps_ref, table, out0, out1, wide, rows):
    taps, frames_out, per_pair, pitch, chunk = dims
    blocks = frames_out + taps - 1
    core = info[1] & 1
    fine = 2 * LANES
    polar = pl.program_id(0)
    for s in range(chunk):
        part = volt[s, 0, 0] if near else volt[s, polar, (info[1] >> 1) ^ plane]
        wide[pl.ds(s * pitch, per_pair), :] = part.astype(jnp.float32)
    for turn, out in ((0, out0), (1, out1)):
        base = jnp.bitwise_xor(core, turn) * (per_pair // 2)
        for q in range(2):
            for half in range(2):
                lane = half * LANES
                coef = [taps_ref[t : t + 1, lane : lane + LANES] for t in range(taps)]
                data = [
                    wide[pl.ds(base + 2 * (2 * i + half) + q, chunk, stride=pitch), :]
                    for i in range(blocks)
                ]
                for m in range(frames_out):
                    total = coef[0] * data[m]
                    for t in range(1, taps):
                        total = total + coef[t] * data[m + t]
                    col = q * fine + lane
                    rows[m * chunk : (m + 1) * chunk, col : col + LANES] = total.astype(
                        rows.dtype
                    )
        first = jnp.dot(rows[:, :fine], table[...], preferred_element_type=jnp.float32)
        second = jnp.dot(rows[:, fine:], table[...], preferred_element_type=jnp.float32)
        real = first[:, :fine] + second[:, fine:]
        imag = second[:, :fine] - first[:, fine:]
        for m in range(frames_out):
            lead = pl.multiple_of((polar * frames_out + m) * fine, LANES)
            here = slice(m * chunk, (m + 1) * chunk)
            out[0, :, pl.ds(lead, fine)] = real[here].astype(jnp.bfloat16)
            out[1, :, pl.ds(lead, fine)] = imag[here].astype(jnp.bfloat16)


def spectra_pair(info, plane, view, filter_taps, table):
    slots, polars, _, per_pair, _ = view.shape
    taps, fine = filter_taps.shape
    frames_out = per_pair // 8 - taps + 1
    pitch = per_pair + 1
    near = plane == 0
    shapes = [jax.ShapeDtypeStruct((2, slots, polars * frames_out * fine), jnp.bfloat16)] * 2
    if near:
        keep = [pltpu.with_memory_space_constraint(x, pltpu.HBM) for x in (view, filter_taps, table)]
        in_specs = [
            pl.BlockSpec(
                (slots, 1, 1, per_pair, LANES), lambda p, info: (0, p, info[1] >> 1, 0, 0)
            ),
            pl.BlockSpec((taps, fine), lambda p, info: (0, 0)),
            pl.BlockSpec((fine, 2 * fine), lambda p, info: (0, 0)),
        ]
    else:
        keep = [view, filter_taps, table]
        in_specs = [VMEM_WHOLE] * 3
    return pl.pallas_call(
        functools.partial(
            spectra_body, (taps, frames_out, per_pair, pitch, slots), plane, near
        ),
        grid_spec=pltpu.PrefetchScalarGridSpec(
            num_scalar_prefetch=1,
            grid=(polars,),
            in_specs=in_specs,
            out_specs=[VMEM_WHOLE] * 2,
            scratch_shapes=[
                pltpu.VMEM((slots * pitch, LANES), jnp.float32),
                pltpu.VMEM((frames_out * slots, 2 * fine), jnp.bfloat16),
            ],
        ),
        out_shape=shapes,
        compiler_params=pltpu.CompilerParams(
            dimension_semantics=("arbitrary",), vmem_limit_bytes=KERNEL_VMEM
        ),
        name="spectra",
    )(info, *keep)


def mask_body(info, count, ids, weights, *refs):
    outs, live = refs[:-1], refs[-1]
    _, freq, slots, _ = weights.shape
    width = outs[0].shape[3]
    known = jnp.broadcast_to(ids[...], (LANES, ids.shape[1])).astype(jnp.float32).T
    live[...] = (known < count[0].astype(jnp.float32)).astype(jnp.float32)
    for j in range(freq):
        place = jnp.bitwise_xor(info[1], j)
        keep = live[pl.ds(pl.multiple_of(place * slots, slots), slots), :][:, :1]
        for d, out in enumerate(outs):
            start = pl.multiple_of(jnp.bitwise_xor(info[0], d) * width, width)
            for q in range(2):
                value = weights[q, place, :, pl.ds(start, width)].astype(jnp.float32)
                out[q, j] = (value * keep).astype(jnp.bfloat16)


def mask_weights(info, ids, count, weights, stn):
    _, freq, slots, beams = weights.shape
    shape = jax.ShapeDtypeStruct((2, freq, slots, beams // stn), jnp.bfloat16)
    smem = pl.BlockSpec(memory_space=pltpu.SMEM)
    vmem = pl.BlockSpec(memory_space=pltpu.VMEM)
    return pl.pallas_call(
        mask_body,
        in_specs=[smem, smem, vmem, vmem],
        out_specs=[vmem] * stn,
        out_shape=[shape] * stn,
        scratch_shapes=[pltpu.VMEM((freq * slots, LANES), jnp.float32)],
        compiler_params=pltpu.CompilerParams(vmem_limit_bytes=KERNEL_VMEM),
        name="mask",
    )(info, count, ids.reshape(1, freq * slots), weights)


def turn_body(cut, *refs):
    parts, outs = refs[:-2], refs[-2:]
    rows = parts[0].shape[1]
    for g, part in enumerate(parts):
        real = part[0].astype(jnp.float32).T.astype(jnp.bfloat16)
        imag = part[1].astype(jnp.float32).T.astype(jnp.bfloat16)
        for out, low, high in ((outs[0], 0, cut), (outs[1], cut, rows)):
            size = high - low
            lead = slice(2 * g * size, (2 * g + 1) * size)
            tail = slice((2 * g + 1) * size, (2 * g + 2) * size)
            out[0, :, lead] = real[:, low:high]
            out[0, :, tail] = -imag[:, low:high]
            out[1, :, lead] = imag[:, low:high]
            out[1, :, tail] = real[:, low:high]


def turn_weights(parts, cut):
    _, rows, width = parts[0].shape
    return pl.pallas_call(
        functools.partial(turn_body, cut),
        out_shape=[
            jax.ShapeDtypeStruct((2, width, 2 * len(parts) * size), jnp.bfloat16)
            for size in (cut, rows - cut)
        ],
        compiler_params=pltpu.CompilerParams(vmem_limit_bytes=KERNEL_VMEM),
        name="turn",
    )(*parts)


def gather_rows(places, pieces, here, data):
    slots = pieces[0].shape[1]
    span = data.shape[0] // (2 * (max(g for g, _ in places) + 1))
    low = min(j for _, j in places)
    for (g, j), piece in zip(places, pieces):
        for q in range(2):
            row = (2 * g + q) * span + (j - low) * slots
            data[row : row + slots, :] = piece[q, :, here]


def columns(tile):
    return pl.ds(pl.multiple_of(pl.program_id(0) * tile, tile), tile)


def early_body(places, tile, weights, *refs):
    pieces, out, data = refs[: len(places)], refs[-2], refs[-1]
    here = columns(tile)
    gather_rows(places, pieces, here, data)
    for q in range(2):
        out[q, :, here] = jnp.dot(
            weights[q], data[...], preferred_element_type=jnp.float32
        )


def late_body(places, shifts, tile, first, pitch, weights, partial, *refs):
    pieces = refs[: len(places)]
    out, data, wide = refs[-3:]
    views = [
        piece.at[:, :, pl.ds(shift * tile, tile)] for piece, shift in zip(pieces, shifts)
    ]
    gather_rows(places, views, slice(None), data)
    beams = weights.shape[1]
    for q in range(2):
        part = partial[q, :, first * tile : (first + 1) * tile] + jnp.dot(
            weights[q], data[...], preferred_element_type=jnp.float32
        )
        for j in range(tile // LANES):
            wide[pl.ds(2 * j + q, beams, stride=pitch), :] = part[
                :, j * LANES : (j + 1) * LANES
            ]
    high = 2 * tile // LANES
    for b in range(beams):
        out[b] = wide[pl.ds(b * pitch, high), :].astype(jnp.bfloat16)


def beam_early(weights, pieces, tile):
    _, beams, depth = weights.shape
    total = pieces[0][2].shape[2]
    return pl.pallas_call(
        functools.partial(early_body, [(g, j) for g, j, _ in pieces], tile),
        grid=(total // tile,),
        in_specs=[VMEM_WHOLE] * (1 + len(pieces)),
        out_specs=VMEM_WHOLE,
        out_shape=jax.ShapeDtypeStruct((2, beams, total), jnp.float32),
        scratch_shapes=[pltpu.VMEM((depth, tile), jnp.bfloat16)],
        compiler_params=pltpu.CompilerParams(
            dimension_semantics=("arbitrary",), vmem_limit_bytes=KERNEL_VMEM
        ),
        name="early",
    )(weights, *[piece for _, _, piece in pieces])


def beam_late(weights, partial, pieces, first, tile, before):
    _, beams, depth = weights.shape
    total = partial.shape[2]
    high = 2 * tile // LANES
    pitch = high + 1
    extra = [] if before is None else [before]
    shifts = [first if piece.shape[2] == total else 0 for _, _, piece in pieces]
    return pl.pallas_call(
        functools.partial(
            late_body, [(g, j) for g, j, _ in pieces], shifts, tile, first, pitch
        ),
        grid=(1,),
        in_specs=[VMEM_WHOLE] * (2 + len(pieces))
        + [pl.BlockSpec(memory_space=pl.ANY)] * len(extra),
        out_specs=pl.BlockSpec((beams, high, LANES), lambda n: (0, first, 0)),
        out_shape=jax.ShapeDtypeStruct((beams, 2 * total // LANES, LANES), jnp.bfloat16),
        input_output_aliases={2 + len(pieces): 0} if extra else {},
        scratch_shapes=[
            pltpu.VMEM((depth, tile), jnp.bfloat16),
            pltpu.VMEM((beams * pitch, LANES), jnp.float32),
        ],
        compiler_params=pltpu.CompilerParams(
            dimension_semantics=("arbitrary",), vmem_limit_bytes=KERNEL_VMEM
        ),
        name="late",
    )(weights, partial, *[piece for _, _, piece in pieces], *extra)


def swap(array, axis, step, size):
    return lax.ppermute(array, axis, [(i, i ^ step) for i in range(size)])


def fast(stn, freq, voltages, filter_taps, beam_weights, station_map, active_counts):
    slots, polars, chans, _, samples = voltages.shape
    taps, fine = filter_taps.shape
    s_me = lax.axis_index("stn")
    f_me = lax.axis_index("freq")

    info = jnp.stack([s_me, f_me]).astype(jnp.int32)
    grouped = beam_weights[0].reshape(2, freq, slots, beam_weights.shape[3])
    wparts = mask_weights(info, station_map, active_counts, grouped, stn)
    wparts = [wparts[0]] + [swap(wparts[d], "stn", d, stn) for d in range(1, stn)]
    w_early, w_late = turn_weights(
        [w.reshape(2, freq * slots, -1) for w in wparts], (freq - 2) * slots
    )

    view = with_layout_constraint(
        voltages.reshape(slots, polars, chans, 2, samples // LANES, LANES),
        Layout((0, 1, 2, 4, 3, 5)),
    )
    view = view.transpose(0, 1, 2, 4, 3, 5).reshape(
        slots, polars, chans // 2, 4 * samples // LANES, LANES
    )
    table = cos_sin(fine)
    planes = freq // 2
    total = polars * (samples - (taps - 1) * fine)
    held = {}
    for jz in range(planes):
        made = spectra_pair(info, jz, view, filter_taps, table)
        for i, piece in enumerate(made):
            j, p = 2 * jz + i % 2, i // 2
            held[j, p] = piece if j == 0 else swap(piece, "freq", j, freq)

    bits = [1 << i for i in range(stn.bit_length() - 1)]
    early, late = [], [[], []]
    tile = total // 2
    for (j, p), piece in held.items():
        have = {0: piece}
        halves = {}
        for i, bit in enumerate(bits if j % 2 == 0 else bits[::-1]):
            for n, (g, a) in enumerate(list(have.items())):
                if j >= freq - 2 and i == len(bits) - 1 and n > 0:
                    parts = [a[:, :, h * tile : (h + 1) * tile] for h in range(2)]
                    halves[g ^ bit] = [swap(part, "stn", bit, stn) for part in parts]
                else:
                    have[g ^ bit] = swap(a, "stn", bit, stn)
        for h in range(2):
            late[h] += [(g, j, a) for g, a in have.items() if j >= freq - 2]
            late[h] += [(g, j, a[h]) for g, a in halves.items()]
        early += [(g, j, a) for g, a in have.items() if j < freq - 2]

    partial = beam_early(w_early, early, 4 * LANES)
    out = None
    for h in range(2):
        out = beam_late(w_late, partial, late[h], h, tile, out)
    high = out.shape[1] // 2
    return out.reshape(out.shape[0], high, 2, LANES).transpose(0, 2, 1, 3).reshape(
        out.shape[0], 2, 1, high * LANES
    )


def solution(mesh):
    placed = (
        P(("stn", "freq"), None, None, None, None),
        P(),
        P("freq", None, "stn", None),
        P("stn"),
        P("freq"),
    )
    stn, freq = mesh.shape["stn"], mesh.shape["freq"]

    def per_device(voltages, filter_taps, beam_weights, station_map, active_counts):
        args = (voltages, filter_taps, beam_weights, station_map, active_counts)
        if voltages.shape[0] % 16 or active_counts.shape[0] != 1:
            return plain(*args)
        return fast(stn, freq, *args)

    return jax.shard_map(
        per_device,
        mesh=mesh,
        in_specs=placed,
        out_specs=P("stn", None, "freq", None),
        check_vma=False,
    )
```
